32 devices in a mesh: shots: 2 (over y), bx: 4 (over z), by: 2 (over x), bz: 2 (over core).
Axes of the slice: x: 2, y: 2, z: 4, core: 2. Of those that a mesh axis runs over, the one named last changes fastest.
Arguments:
- weights: bfloat16 [16384, 2, 256], P(('shots', 'bx', 'by', 'bz')), parts along dimension 0, may hold values from -6 to 6
- interp: bfloat16 [2, 2, 256, 256], replicated, may hold values from -0.25 to 0.25
- slowness: float32 [2, 2, 256], replicated, may hold values from -0.05 to 0.05
- box_coord: int32 [2, 8192], P(None, ('bx', 'by', 'bz')), may hold values from 0 to 127
Outputs:
- result: bfloat16 [16384, 2, 256], P(('shots', 'bx', 'by', 'bz')), parts along dimension 0
The draws below stay inside these ranges and needn't reach their ends.
There are 2 independent parts, one for each index of `shots`. The reference program is written for one: setup_inputs(seed, part) draws one part's arguments, and reference() takes and returns one part's arrays. A program takes and returns all parts, laid end to end along the dimension named above; an argument that names none is the same for every part. Nothing has to cross between parts.
All inputs are finite; a program needn't handle non-finite values.
Results may differ from the reference program's by a relative error of at most 0.022.
Values may be sent and summed in bfloat16 or wider, within the bound.
No kernel may reach another device: no remote copies, remote signals or barrier semaphores. Data moves between devices by JAX's collectives and lax.ppermute only.
A program may use at most 64 MiB of HBM per device.

```python
import jax
import jax.numpy as jnp

RANK = 256
SLOTS_DEV = 512
LOCAL = 4
BOXES = 128
SLOTS = 8192
N_BX = 4
N_BY = 2
N_BZ = 2


def touch_ends(entries, own_key, least, largest):
    dims = entries.shape
    index_at = [jax.random.randint(jax.random.fold_in(own_key, axis), (), 0, dims[axis]) for axis in range(len(dims))]
    entries = entries.at[tuple(index_at)].set(least)
    longest = dims.index(max(dims))
    index_at[longest] = (index_at[longest] + 1) % dims[longest]
    return entries.at[tuple(index_at)].set(largest)


def shard_levels(rng, extent, shards, low, top_value):
    gain = 1.0
    for position, shards_of in shards:
        heights = jax.random.uniform(jax.random.fold_in(jax.random.fold_in(rng, 6), position), (shards_of,), jnp.float32, low / len(shards), top_value / len(shards))
        gain = gain * jnp.repeat(jnp.exp(heights), extent[position] // shards_of).reshape((-1,) + (1,) * (len(extent) - 1 - position))
    return gain


def normal_values(own_key, shape, deviation, limit, cuts=(), dtype=jnp.bfloat16):
    entries = jax.random.normal(own_key, shape, jnp.float32) * deviation
    if len(cuts) > 0:
        entries = shard_levels(own_key, shape, cuts, -0.22, 0.18) * entries
    return jnp.clip(entries, min=-limit, max=limit).astype(dtype)


def setup_inputs(seed: int = 0, part: int = 0) -> dict:
    key_list = jax.random.split(jax.random.key(seed), 5)
    part_keys = jax.random.split(jax.random.fold_in(key_list[4], part), 5)
    return {
        "weights": normal_values(part_keys[0], (SLOTS, 2, RANK), 1.0, 6.0, ((0, 16),)),
        "interp": normal_values(key_list[1], (2, 2, RANK, RANK), (2 * RANK) ** -0.5, 0.25),
        "slowness": jnp.clip(jax.random.uniform(key_list[2], (2, 2, RANK), jnp.float32, -0.05, 0.05), -0.05, 0.05),
        "box_coord": touch_ends(jax.random.randint(key_list[3], (2, SLOTS), 0, BOXES), jax.random.fold_in(key_list[3], 1), 0, BOXES - 1).astype(jnp.int32),
    }


def apply_matrix(block, matrix):
    block_shape = block.shape
    product = jnp.dot(block.reshape(-1, block_shape[-1]), matrix, preferred_element_type=jnp.float32)
    return product.reshape(block_shape)


def rotate_phase(summed, cosine, sine):
    real_part = summed[..., 0, :]
    imag_part = summed[..., 1, :]
    return jnp.stack([cosine * real_part - sine * imag_part, sine * real_part + cosine * imag_part], axis=-2).astype(jnp.bfloat16)


def level_step(grouped, interp, cos_group, sin_group):
    first_child = grouped[:, 0]
    second_child = grouped[:, 1]
    results = []
    for target in range(2):
        summed = apply_matrix(first_child, interp[target, 0]) + apply_matrix(second_child, interp[target, 1])
        results.append(rotate_phase(summed, cos_group[:, target], sin_group[:, target]))
    return jnp.stack(results, axis=1)


def reference(weights, interp, slowness, box_coord):
    groups = N_BX * N_BY * N_BZ
    per_dev = SLOTS_DEV
    coords = box_coord.astype(jnp.float32)
    dist_angle = coords[0][:, None] * slowness[0, 0][None, :] + coords[1][:, None] * slowness[0, 1][None, :]
    local_angle = coords[0][:, None] * slowness[1, 0][None, :] + coords[1][:, None] * slowness[1, 1][None, :]
    dist_cos = jnp.cos(dist_angle)
    dist_sin = jnp.sin(dist_angle)
    local_cos = jnp.cos(local_angle)
    local_sin = jnp.sin(local_angle)
    current = weights
    bit_count = groups.bit_length() - 1
    for bit_num in range(bit_count):
        spread = 2 ** bit_num
        outer = groups // (2 * spread)
        grouped = current.reshape(outer, 2, spread * per_dev, 2, RANK)
        cos_group = dist_cos.reshape(outer, 2, spread * per_dev, RANK)
        sin_group = dist_sin.reshape(outer, 2, spread * per_dev, RANK)
        current = level_step(grouped, interp, cos_group, sin_group).reshape(-1, 2, RANK)
    for local_num in range(LOCAL):
        span_len = per_dev >> (local_num + 1)
        grouped = current.reshape(-1, 2, span_len, 2, RANK)
        cos_group = local_cos.reshape(-1, 2, span_len, RANK)
        sin_group = local_sin.reshape(-1, 2, span_len, RANK)
        current = level_step(grouped, interp, cos_group, sin_group).reshape(-1, 2, RANK)
    return current
```

```python
import functools

import jax
import jax.numpy as jnp
from jax import lax
from jax.experimental import pallas as pl
from jax.experimental.pallas import tpu as pltpu
from jax.sharding import PartitionSpec as P

LOCAL = 4
TILE = 8


def from_partner(block, axis, stride):
    count = lax.axis_size(axis)
    route = []
    for low in range(count):
        high = low | 1 << stride
        if high != low and high < count:
            route += [(low, high), (high, low)]
    return lax.ppermute(block, axis, route)


def apply_matrix(block, matrix):
    block_shape = block.shape
    product = jnp.dot(
        block.reshape(-1, block_shape[-1]), matrix, preferred_element_type=jnp.float32
    )
    return product.reshape(block_shape)


def rotate_phase(summed, cosine, sine):
    real_part = summed[..., 0, :]
    imag_part = summed[..., 1, :]
    return jnp.stack(
        [cosine * real_part - sine * imag_part, sine * real_part + cosine * imag_part], axis=-2
    ).astype(jnp.bfloat16)


def level_step(grouped, interp, cos_group, sin_group):
    first_child = grouped[:, 0]
    second_child = grouped[:, 1]
    results = []
    for target in range(2):
        summed = apply_matrix(first_child, interp[target, 0]) + apply_matrix(
            second_child, interp[target, 1]
        )
        results.append(rotate_phase(summed, cos_group[:, target], sin_group[:, target]))
    return jnp.stack(results, axis=1)


def partner_step(current, partner, upper_bit, interp, cosine, sine):
    mine_part = apply_matrix(current, interp[upper_bit, upper_bit])
    other_part = apply_matrix(partner, interp[upper_bit, 1 - upper_bit])
    return rotate_phase(mine_part + other_part, cosine, sine)


def general(weights, interp, slowness, box_coord):
    per_dev = weights.shape[0]
    rank_size = weights.shape[2]
    coords = box_coord.astype(jnp.float32)
    dist_angle = (
        coords[0][:, None] * slowness[0, 0][None, :] + coords[1][:, None] * slowness[0, 1][None, :]
    )
    local_angle = (
        coords[0][:, None] * slowness[1, 0][None, :] + coords[1][:, None] * slowness[1, 1][None, :]
    )
    dist_cos = jnp.cos(dist_angle)
    dist_sin = jnp.sin(dist_angle)
    local_cos = jnp.cos(local_angle)
    local_sin = jnp.sin(local_angle)
    current = weights
    for axis in ("bz", "by", "bx"):
        for bit_num in range(lax.axis_size(axis).bit_length() - 1):
            partner = from_partner(current, axis, bit_num)
            upper_bit = lax.axis_index(axis) >> bit_num & 1
            current = partner_step(current, partner, upper_bit, interp, dist_cos, dist_sin)
    for local_num in range(LOCAL):
        span_len = per_dev >> local_num + 1
        grouped = current.reshape(-1, 2, span_len, 2, rank_size)
        cos_group = local_cos.reshape(-1, 2, span_len, rank_size)
        sin_group = local_sin.reshape(-1, 2, span_len, rank_size)
        current = level_step(grouped, interp, cos_group, sin_group).reshape(per_dev, 2, rank_size)
    return current


def rows_of(value):
    return value.reshape(-1, value.shape[-1])


def tiles_of(value):
    return value.reshape(-1, TILE, value.shape[-1])


def swap_parts(tiles):
    row = lax.broadcasted_iota(jnp.int32, tiles.shape, 1)
    return jnp.where(
        row % 2 == 0, pltpu.roll(tiles, TILE - 1, axis=1), pltpu.roll(tiles, 1, axis=1)
    )


def rotate_tiles(summed, cosine, sine):
    return cosine * summed + sine * swap_parts(summed)


def angles_of(coords, slow, count):
    parts = []
    for h in range(count):
        parts.append(
            coords[:, h : h + 1] * slow[0:1, :] + coords[:, count + h : count + h + 1] * slow[1:2, :]
        )
    return jnp.stack(parts)


def phase_tables(coords, slow, count):
    angle = angles_of(coords, slow, count)
    row = lax.broadcasted_iota(jnp.int32, angle.shape, 1)
    sine = jnp.sin(angle)
    return jnp.cos(angle), jnp.where(row % 2 == 0, -sine, sine)


def own_table_kernel(highs, coord_ref, slow_ref, cos_ref, sin_ref):
    for d in range(coord_ref.shape[0]):
        cosine, sine = phase_tables(coord_ref[d].astype(jnp.float32), slow_ref[0], highs)
        cos_ref[:, d] = cosine
        sin_ref[:, d] = sine


def table_kernel(highs, msg_ref, slow_ref, *out_refs):
    coords = msg_ref[highs].astype(jnp.float32)
    for table in range(2):
        cosine, sine = phase_tables(coords, slow_ref[table], highs)
        out_refs[2 * table][...] = cosine
        out_refs[2 * table + 1][...] = sine


def first_kernel(
    count, highs, at_ref, own_ref, other_ref, interp_ref, cos_ref, sin_ref, coord_ref, *rest
):
    out_refs, held = rest[:count], rest[count]
    me, upper = at_ref[0], at_ref[1]
    rank = own_ref.shape[1]
    summed = jnp.dot(
        own_ref[...], interp_ref[upper, upper], preferred_element_type=jnp.float32
    ) + jnp.dot(other_ref[...], interp_ref[upper, 1 - upper], preferred_element_type=jnp.float32)
    shape = (highs * count, TILE, rank)
    turned = rotate_tiles(
        tiles_of(summed), cos_ref[...].reshape(shape), sin_ref[...].reshape(shape)
    )
    held[...] = turned.reshape(highs, count, TILE, rank)
    for k in range(count):
        to = jnp.bitwise_xor(me, k)
        out_refs[k][0:highs] = held[:, to].astype(jnp.bfloat16)
        out_refs[k][highs] = coord_ref[to]


def levels_kernel(count, highs, at_ref, interp_ref, *rest):
    msg_refs = rest[:count]
    table_refs = rest[count : 5 * count]
    out_refs = rest[5 * count : 6 * count]
    held = rest[6 * count]
    me = at_ref[0]
    rank = interp_ref.shape[-1]
    bits = count.bit_length() - 1

    def table(which, k):
        return table_refs[4 * k + which][...]

    def mix(first, second, left, right):
        return jnp.dot(first, left, preferred_element_type=jnp.float32) + jnp.dot(
            second, right, preferred_element_type=jnp.float32
        )

    for k in range(count):
        held[k] = msg_refs[k][0:highs].astype(jnp.float32)
    for bit in range(bits):
        mine = jnp.right_shift(me, bit) & 1
        lows = [k for k in range(count) if not k >> bit & 1]
        ups = [k | 1 << bit for k in lows]
        first = jnp.concatenate([rows_of(held[k]) for k in lows]).astype(jnp.bfloat16)
        second = jnp.concatenate([rows_of(held[k]) for k in ups]).astype(jnp.bfloat16)
        for ks, upper, near, far in ((lows, mine, first, second), (ups, 1 - mine, second, first)):
            summed = mix(near, far, interp_ref[upper, upper], interp_ref[upper, 1 - upper])
            summed = summed.reshape(len(ks), highs, TILE, rank)
            for at, k in enumerate(ks):
                held[k] = rotate_tiles(summed[at], table(0, k), table(1, k))
    for level in range(LOCAL):
        span = highs >> level + 1
        groups = [[h for h in range(highs) if (h // span) % 2 == t] for t in range(2)]
        children = []
        for t in range(2):
            tiles = [held[k, h] for k in range(count) for h in groups[t]]
            children.append(jnp.concatenate(tiles).astype(jnp.bfloat16))
        for t in range(2):
            summed = mix(children[0], children[1], interp_ref[t, 0], interp_ref[t, 1])
            summed = summed.reshape(count, highs // 2, TILE, rank)
            for k in range(count):
                cosine = jnp.stack([table_refs[4 * k + 2][h] for h in groups[t]])
                sine = jnp.stack([table_refs[4 * k + 3][h] for h in groups[t]])
                turned = rotate_tiles(summed[k], cosine, sine)
                for at, h in enumerate(groups[t]):
                    if level == LOCAL - 1:
                        out_refs[k][h] = turned[at].astype(jnp.bfloat16)
                    else:
                        held[k, h] = turned[at]


def gather_kernel(count, at_ref, *rest):
    back_refs, out_ref = rest[:count], rest[count]
    for k in range(count):
        out_ref[:, jnp.bitwise_xor(at_ref[0], k)] = back_refs[k][...]


def transposed(weights, interp, slowness, box_coord):
    per_dev, parts, rank = weights.shape
    count = lax.axis_size("bx") * lax.axis_size("by")
    highs = 1 << LOCAL
    lows = per_dev // highs // count
    me = lax.axis_index("bx") * lax.axis_size("by") + lax.axis_index("by")
    upper = lax.axis_index("bz")
    at = jnp.stack([me, upper]).astype(jnp.int32)
    bf16, f32 = jnp.bfloat16, jnp.float32
    vmem = pl.BlockSpec(memory_space=pltpu.VMEM)
    smem = pl.BlockSpec(memory_space=pltpu.SMEM)

    def call(kernel, name, in_specs, outs, scratch=(), flops=0, moved=0):
        return pl.pallas_call(
            kernel,
            name=name,
            in_specs=in_specs,
            out_specs=[vmem] * len(outs),
            out_shape=[jax.ShapeDtypeStruct(s, t) for s, t in outs],
            scratch_shapes=list(scratch),
            cost_estimate=pl.CostEstimate(flops=flops, bytes_accessed=moved, transcendentals=0),
        )

    def swap_with(block, axes, mask):
        size = 1
        for axis in axes:
            size *= lax.axis_size(axis)
        return lax.ppermute(block, axes, [(i, i ^ mask) for i in range(size)])

    coord = box_coord.astype(bf16).reshape(2, highs, count, lows).transpose(2, 3, 0, 1)
    coord = jnp.broadcast_to(coord[:, :, None], (count, lows, parts, 2, highs))
    coord = coord.reshape(count, TILE, 2 * highs)
    coord = jnp.pad(coord, ((0, 0), (0, 0), (0, rank - 2 * highs)))

    other = swap_with(weights, ("bz",), 1)
    table_shape = (highs, count, TILE, rank)
    own_cos, own_sin = call(
        functools.partial(own_table_kernel, highs),
        "own_table",
        [vmem, vmem],
        [(table_shape, f32)] * 2,
        flops=1 << 24,
        moved=1 << 21,
    )(coord, slowness)
    flat = (per_dev * parts, rank)
    messages = call(
        functools.partial(first_kernel, count, highs),
        "first_level",
        [smem] + [vmem] * 6,
        [((highs + 1, TILE, rank), bf16)] * count,
        [pltpu.VMEM(table_shape, f32)],
        flops=1 << 28,
        moved=1 << 21,
    )(at, weights.reshape(flat), other.reshape(flat), interp, own_cos, own_sin, coord)

    order = [4, 1, 6, 2, 5, 3, 7]
    arrived = [messages[0]] + [None] * (count - 1)
    for k in order:
        arrived[k] = swap_with(messages[k], ("bx", "by"), k)
    tables = []
    for k in range(count):
        tables += call(
            functools.partial(table_kernel, highs),
            "phase_table",
            [vmem, vmem],
            [((highs, TILE, rank), f32)] * 4,
            flops=1 << 22,
            moved=1 << 19,
        )(arrived[k], slowness)
    results = call(
        functools.partial(levels_kernel, count, highs),
        "levels",
        [smem] + [vmem] * (1 + 5 * count),
        [((highs, TILE, rank), bf16)] * count,
        [pltpu.VMEM((count, highs, TILE, rank), f32)],
        flops=1 << 31,
        moved=1 << 22,
    )(at, interp, *arrived, *tables)
    back = [results[0]] + [None] * (count - 1)
    for k in order:
        back[k] = swap_with(results[k], ("bx", "by"), k)
    (gathered,) = call(
        functools.partial(gather_kernel, count),
        "gather",
        [smem] + [vmem] * count,
        [(table_shape, bf16)],
        moved=1 << 20,
    )(at, *back)
    return gathered.reshape(per_dev, parts, rank)


def local(weights, interp, slowness, box_coord):
    count = lax.axis_size("bx") * lax.axis_size("by")
    small = lax.axis_size("bz") == 2 and count == 8
    if small and weights.shape[0] * weights.shape[1] == (TILE * count) << LOCAL:
        return transposed(weights, interp, slowness, box_coord)
    return general(weights, interp, slowness, box_coord)


def solution(mesh):
    placed = (P(("shots", "bx", "by", "bz"), None, None), P(), P(), P(None, ("bx", "by", "bz")))
    return jax.shard_map(
        local,
        mesh=mesh,
        in_specs=placed,
        out_specs=P(("shots", "bx", "by", "bz"), None, None),
        check_vma=False,
    )
```

```python
import functools

import jax
import jax.numpy as jnp
from jax import lax
from jax.experimental import pallas as pl
from jax.experimental.pallas import tpu as pltpu
from jax.sharding import PartitionSpec as P


LOCAL = 4
TILE = 8
ORDER = (4, 5, 6, 7, 2, 1, 3)


def from_partner(block, axis, stride):
    count = lax.axis_size(axis)
    route = []
    for low in range(count):
        high = low | 1 << stride
        if high != low and high < count:
            route += [(low, high), (high, low)]
    return lax.ppermute(block, axis, route)


def apply_matrix(block, matrix):
    block_shape = block.shape
    product = jnp.dot(
        block.reshape(-1, block_shape[-1]), matrix, preferred_element_type=jnp.float32
    )
    return product.reshape(block_shape)


def rotate_phase(summed, cosine, sine):
    real_part = summed[..., 0, :]
    imag_part = summed[..., 1, :]
    return jnp.stack(
        [cosine * real_part - sine * imag_part, sine * real_part + cosine * imag_part], axis=-2
    ).astype(jnp.bfloat16)


def level_step(grouped, interp, cos_group, sin_group):
    first_child = grouped[:, 0]
    second_child = grouped[:, 1]
    results = []
    for target in range(2):
        summed = apply_matrix(first_child, interp[target, 0]) + apply_matrix(
            second_child, interp[target, 1]
        )
        results.append(rotate_phase(summed, cos_group[:, target], sin_group[:, target]))
    return jnp.stack(results, axis=1)


def partner_step(current, partner, upper_bit, interp, cosine, sine):
    mine_part = apply_matrix(current, interp[upper_bit, upper_bit])
    other_part = apply_matrix(partner, interp[upper_bit, 1 - upper_bit])
    return rotate_phase(mine_part + other_part, cosine, sine)


def general(weights, interp, slowness, box_coord):
    per_dev = weights.shape[0]
    rank_size = weights.shape[2]
    coords = box_coord.astype(jnp.float32)
    dist_angle = (
        coords[0][:, None] * slowness[0, 0][None, :] + coords[1][:, None] * slowness[0, 1][None, :]
    )
    local_angle = (
        coords[0][:, None] * slowness[1, 0][None, :] + coords[1][:, None] * slowness[1, 1][None, :]
    )
    dist_cos = jnp.cos(dist_angle)
    dist_sin = jnp.sin(dist_angle)
    local_cos = jnp.cos(local_angle)
    local_sin = jnp.sin(local_angle)
    current = weights
    for axis in ("bz", "by", "bx"):
        for bit_num in range(lax.axis_size(axis).bit_length() - 1):
            partner = from_partner(current, axis, bit_num)
            upper_bit = lax.axis_index(axis) >> bit_num & 1
            current = partner_step(current, partner, upper_bit, interp, dist_cos, dist_sin)
    for local_num in range(LOCAL):
        span_len = per_dev >> local_num + 1
        grouped = current.reshape(-1, 2, span_len, 2, rank_size)
        cos_group = local_cos.reshape(-1, 2, span_len, rank_size)
        sin_group = local_sin.reshape(-1, 2, span_len, rank_size)
        current = level_step(grouped, interp, cos_group, sin_group).reshape(per_dev, 2, rank_size)
    return current


def rows_of(value):
    return value.reshape(-1, value.shape[-1])


def tiles_of(value):
    return value.reshape(-1, TILE, value.shape[-1])


def swap_parts(tiles):
    row = lax.broadcasted_iota(jnp.int32, tiles.shape, 1)
    return jnp.where(
        row % 2 == 0, pltpu.roll(tiles, TILE - 1, axis=1), pltpu.roll(tiles, 1, axis=1)
    )


def rotate_tiles(summed, cosine, sine):
    return cosine * summed + sine * swap_parts(summed)


def sin_cos(angle):
    quarter = jnp.floor(angle * 0.6366197723675814 + 0.5)
    rest = angle - quarter * 1.5703125
    rest = rest - quarter * 4.837512969970703e-4
    rest = rest - quarter * 7.549789948768648e-8
    square = rest * rest
    odd_part = (-1.9515295891e-4 * square + 8.3321608736e-3) * square - 1.6666654611e-1
    odd_part = odd_part * square * rest + rest
    even_part = (2.443315711809948e-5 * square - 1.388731625493765e-3) * square
    even_part = (even_part + 4.166664568298827e-2) * square * square - 0.5 * square + 1.0
    turn = quarter.astype(jnp.int32)
    odd = (turn & 1) != 0
    sine = jnp.where(odd, even_part, odd_part)
    cosine = jnp.where(odd, odd_part, even_part)
    return (
        jnp.where((turn & 2) != 0, -sine, sine),
        jnp.where(((turn + 1) & 2) != 0, -cosine, cosine),
    )


def even_rows(shape):
    return lax.broadcasted_iota(jnp.int32, shape, len(shape) - 2) % 2 == 0


def paired_tables(coords, slow_x, slow_y, count):
    angle = jnp.stack(
        [
            coords[:, h : h + 1] * slow_x + coords[:, count + h : count + h + 1] * slow_y
            for h in range(count)
        ]
    )
    sine, cosine = sin_cos(angle)
    even = even_rows(angle.shape)
    return (
        jnp.where(even, cosine, pltpu.roll(cosine, 1, axis=1)),
        jnp.where(even, -sine, pltpu.roll(sine, 1, axis=1)),
        jnp.where(even, pltpu.roll(cosine, TILE - 1, axis=1), cosine),
        jnp.where(even, -pltpu.roll(sine, TILE - 1, axis=1), sine),
    )


def own_table_kernel(
    count, highs, box_ref, slow_ref, interp_ref, coord_ref, cos_ref, sin_ref, matrix_ref
):
    slots = box_ref.shape[1]
    rank = slow_ref.shape[-1]
    low_count = slots // highs
    rows = count * TILE
    slot = lax.broadcasted_iota(jnp.int32, (rows, slots), 1)
    row = lax.broadcasted_iota(jnp.int32, (rows, slots), 0)
    mine = slot % low_count == row // (rows // low_count)
    high = lax.broadcasted_iota(jnp.int32, (slots, rank), 0) // low_count
    column = lax.broadcasted_iota(jnp.int32, (slots, rank), 1)
    coords = jnp.zeros((rows, rank), jnp.float32)
    for which in range(2):
        picked = jnp.where(mine, box_ref[which : which + 1].astype(jnp.float32), 0.0)
        fold = jnp.where(column == high + which * highs, 1.0, 0.0).astype(jnp.bfloat16)
        coords += jnp.dot(picked.astype(jnp.bfloat16), fold, preferred_element_type=jnp.float32)
    coords = coords.reshape(count, TILE, rank)
    coord_ref[...] = coords.astype(jnp.bfloat16)
    matrix_ref[...] = interp_ref[...]
    slow_x = jnp.broadcast_to(slow_ref[0, 0:1], (TILE, rank))
    slow_y = jnp.broadcast_to(slow_ref[0, 1:2], (TILE, rank))
    half = count // 2
    for d in range(half):
        pair = jnp.where(even_rows((TILE, rank)), coords[d], coords[d + half])
        tables = paired_tables(pair, slow_x, slow_y, highs)
        cos_ref[:, d], sin_ref[:, d] = tables[0], tables[1]
        cos_ref[:, d + half], sin_ref[:, d + half] = tables[2], tables[3]


def table_kernel(highs, msg_ref, slow_ref, *out_refs):
    even = even_rows((TILE, slow_ref.shape[-1]))
    slow_x = jnp.where(even, slow_ref[0, 0:1], slow_ref[1, 0:1])
    slow_y = jnp.where(even, slow_ref[0, 1:2], slow_ref[1, 1:2])
    tables = paired_tables(msg_ref[highs].astype(jnp.float32), slow_x, slow_y, highs)
    for out_ref, table in zip(out_refs, tables):
        out_ref[...] = table


def mix(near, far, near_matrix, far_matrix):
    return jnp.dot(near, near_matrix, preferred_element_type=jnp.float32) + jnp.dot(
        far, far_matrix, preferred_element_type=jnp.float32
    )


def first_kernel(
    count, highs, at_ref, own_ref, other_ref, interp_ref, cos_ref, sin_ref, coord_ref, *rest
):
    out_refs, held = rest[:count], rest[count]
    me, upper = at_ref[0], at_ref[1]
    rank = own_ref.shape[-1]
    flat = (own_ref.shape[0] * own_ref.shape[1], rank)
    summed = mix(
        own_ref.reshape(flat)[...],
        other_ref.reshape(flat)[...],
        interp_ref[upper, upper],
        interp_ref[upper, 1 - upper],
    )
    shape = (highs * count, TILE, rank)
    turned = rotate_tiles(
        tiles_of(summed), cos_ref[...].reshape(shape), sin_ref[...].reshape(shape)
    )
    held[...] = turned.reshape(highs, count, TILE, rank)
    for k in range(count):
        to = jnp.bitwise_xor(me, k)
        out_refs[k][0:highs] = held[:, to].astype(jnp.bfloat16)
        out_refs[k][highs] = coord_ref[to]


def local_levels(held, ks, highs, interp_ref, tables, out_refs):
    rank = interp_ref.shape[-1]
    for level in range(LOCAL):
        span = highs >> level + 1
        groups = [[h for h in range(highs) if (h // span) % 2 == t] for t in range(2)]
        children = []
        for t in range(2):
            tiles = [held[at, h] for at in range(len(ks)) for h in groups[t]]
            children.append(jnp.concatenate(tiles).astype(jnp.bfloat16))
        for t in range(2):
            summed = mix(children[0], children[1], interp_ref[t, 0], interp_ref[t, 1])
            summed = summed.reshape(len(ks), highs // 2, TILE, rank)
            for at in range(len(ks)):
                cos_ref, sin_ref = tables[at]
                cosine = jnp.stack([cos_ref[h] for h in groups[t]])
                sine = jnp.stack([sin_ref[h] for h in groups[t]])
                turned = rotate_tiles(summed[at], cosine, sine)
                for place, h in enumerate(groups[t]):
                    if level == LOCAL - 1:
                        out_refs[at][h] = turned[place].astype(jnp.bfloat16)
                    else:
                        held[at, h] = turned[place]


def device_kernel(count, highs, at_ref, interp_ref, *rest):
    msg_refs, table_refs, rest = rest[:count], rest[count : 5 * count], rest[5 * count :]
    half = count // 2
    far_refs, near_ref, held, far = rest[:half], rest[half], rest[half + 1], rest[half + 2]
    me = at_ref[0]
    rank = interp_ref.shape[-1]
    bits = count.bit_length() - 1
    for k in range(count):
        held[k] = msg_refs[k][0:highs].astype(jnp.float32)
    for bit in range(bits):
        mine = jnp.right_shift(me, bit) & 1
        lows = [k for k in range(count) if not k >> bit & 1]
        ups = [k | 1 << bit for k in lows]
        first = jnp.concatenate([rows_of(held[k]) for k in lows]).astype(jnp.bfloat16)
        second = jnp.concatenate([rows_of(held[k]) for k in ups]).astype(jnp.bfloat16)
        for ks, upper, near, other in ((lows, mine, first, second), (ups, 1 - mine, second, first)):
            summed = mix(near, other, interp_ref[upper, upper], interp_ref[upper, 1 - upper])
            summed = summed.reshape(len(ks), highs, TILE, rank)
            for at, k in enumerate(ks):
                turned = rotate_tiles(summed[at], table_refs[4 * k][...], table_refs[4 * k + 1][...])
                if bit < bits - 1:
                    held[k] = turned
                elif k < half:
                    near_ref[k] = turned
                else:
                    far[k - half] = turned
    tables = [(table_refs[4 * k + 2], table_refs[4 * k + 3]) for k in range(half, count)]
    local_levels(far, range(half, count), highs, interp_ref, tables, far_refs)


def near_kernel(half, highs, interp_ref, near_ref, *rest):
    table_refs, out_refs, held = rest[: 2 * half], rest[2 * half : 3 * half], rest[3 * half]
    held[...] = near_ref[...]
    tables = [(table_refs[2 * k], table_refs[2 * k + 1]) for k in range(half)]
    local_levels(held, range(half), highs, interp_ref, tables, out_refs)


def gather_kernel(count, highs, at_ref, *rest):
    back_refs, out_ref = rest[:count], rest[count]
    rank = out_ref.shape[-1]
    flat = out_ref.reshape(highs * count * TILE, rank)
    for k in range(count):
        place = jnp.bitwise_xor(at_ref[0], k)
        for h in range(highs):
            start = pl.multiple_of((h * count + place) * TILE, TILE)
            flat[pl.ds(start, TILE), :] = back_refs[k][h]


def transposed(weights, interp, slowness, box_coord):
    per_dev, parts, rank = weights.shape
    count = lax.axis_size("bx") * lax.axis_size("by")
    half = count // 2
    highs = 1 << LOCAL
    me = lax.axis_index("bx") * lax.axis_size("by") + lax.axis_index("by")
    upper = lax.axis_index("bz")
    at = jnp.stack([me, upper]).astype(jnp.int32)
    bf16, f32 = jnp.bfloat16, jnp.float32
    vmem = pl.BlockSpec(memory_space=pltpu.VMEM)
    smem = pl.BlockSpec(memory_space=pltpu.SMEM)

    def call(kernel, in_specs, outs, scratch=(), flops=0, moved=0, room=12):
        return pl.pallas_call(
            kernel,
            in_specs=in_specs,
            out_specs=[vmem] * len(outs),
            out_shape=[jax.ShapeDtypeStruct(s, t) for s, t in outs],
            scratch_shapes=list(scratch),
            compiler_params=pltpu.CompilerParams(vmem_limit_bytes=room << 20),
            cost_estimate=pl.CostEstimate(flops=flops, bytes_accessed=moved, transcendentals=0),
        )

    def run(kernel, in_specs, outs, args, **options):
        return call(kernel, in_specs, outs, **options)(*args)

    def swap_with(block, axes, mask):
        size = 1
        for axis in axes:
            size *= lax.axis_size(axis)
        return lax.ppermute(block, axes, [(i, i ^ mask) for i in range(size)])

    other = swap_with(weights, ("bz",), 1)
    table_shape = (highs, count, TILE, rank)
    coord, own_cos, own_sin, matrices = run(
        functools.partial(own_table_kernel, count, highs),
        [vmem] * 3,
        [((count, TILE, rank), bf16)] + [(table_shape, f32)] * 2 + [(interp.shape, bf16)],
        (box_coord, slowness, interp),
        flops=1 << 24,
        moved=1 << 21,
        room=6,
    )
    messages = run(
        functools.partial(first_kernel, count, highs),
        [smem] + [vmem] * 6,
        [((highs + 1, TILE, rank), bf16)] * count,
        (at, weights, other, matrices, own_cos, own_sin, coord),
        scratch=[pltpu.VMEM(table_shape, f32)],
        flops=1 << 28,
        moved=1 << 21,
    )
    arrived = [messages[0]] + [None] * (count - 1)
    for k in ORDER:
        arrived[k] = swap_with(messages[k], ("bx", "by"), k)
    tables = [None] * count
    for k in (0,) + ORDER:
        tables[k] = run(
            functools.partial(table_kernel, highs),
            [vmem, vmem],
            [((highs, TILE, rank), f32)] * 4,
            (arrived[k], slowness),
            flops=1 << 22,
            moved=1 << 19,
            room=6,
        )
    tile_shape = (highs, TILE, rank)
    *far, near = run(
        functools.partial(device_kernel, count, highs),
        [smem] + [vmem] * (1 + 5 * count),
        [(tile_shape, bf16)] * half + [((half,) + tile_shape, f32)],
        (at, matrices, *arrived, *[t for k in range(count) for t in tables[k]]),
        scratch=[pltpu.VMEM((count,) + tile_shape, f32), pltpu.VMEM((half,) + tile_shape, f32)],
        flops=1 << 31,
        moved=1 << 22,
    )
    close = run(
        functools.partial(near_kernel, half, highs),
        [vmem] * (2 + 2 * half),
        [(tile_shape, bf16)] * half,
        (matrices, near, *[t for k in range(half) for t in tables[k][2:]]),
        scratch=[pltpu.VMEM((half,) + tile_shape, f32)],
        flops=1 << 30,
        moved=1 << 21,
    )
    results = list(close) + list(far)
    back = [results[0]] + [None] * (count - 1)
    for k in ORDER:
        back[k] = swap_with(results[k], ("bx", "by"), k)
    (gathered,) = run(
        functools.partial(gather_kernel, count, highs),
        [smem] + [vmem] * count,
        [((per_dev, parts, rank), bf16)],
        (at, *back),
        moved=1 << 20,
    )
    return gathered


def fits(mesh_shape):
    return mesh_shape["bx"] * mesh_shape["by"] == 8 and mesh_shape["bz"] == 2


def local(weights, interp, slowness, box_coord):
    sizes = {axis: lax.axis_size(axis) for axis in ("bx", "by", "bz")}
    if fits(sizes) and weights.shape[0] * weights.shape[1] == (TILE * 8) << LOCAL:
        return transposed(weights, interp, slowness, box_coord)
    return general(weights, interp, slowness, box_coord)


def solution(mesh):
    placed = (P(("shots", "bx", "by", "bz"), None, None), P(), P(), P(None, ("bx", "by", "bz")))
    return jax.shard_map(
        local,
        mesh=mesh,
        in_specs=placed,
        out_specs=P(("shots", "bx", "by", "bz"), None, None),
        check_vma=False,
    )
```

```python
import functools

import jax
import jax.numpy as jnp
from jax import lax
from jax.experimental import pallas as pl
from jax.experimental.pallas import tpu as pltpu
from jax.sharding import PartitionSpec as P


LOCAL = 4
TILE = 8
RAW = (4, 5, 6)
MIXED = (0, 1, 2, 3, 7)
FINALS = {"final_a": (4, 5, 6, 7), "final_c": (0, 1, 2, 3)}


def from_partner(block, axis, stride):
    count = lax.axis_size(axis)
    route = []
    for low in range(count):
        high = low | 1 << stride
        if high != low and high < count:
            route += [(low, high), (high, low)]
    return lax.ppermute(block, axis, route)


def apply_matrix(block, matrix):
    block_shape = block.shape
    product = jnp.dot(
        block.reshape(-1, block_shape[-1]), matrix, preferred_element_type=jnp.float32
    )
    return product.reshape(block_shape)


def rotate_phase(summed, cosine, sine):
    real_part = summed[..., 0, :]
    imag_part = summed[..., 1, :]
    return jnp.stack(
        [cosine * real_part - sine * imag_part, sine * real_part + cosine * imag_part], axis=-2
    ).astype(jnp.bfloat16)


def level_step(grouped, interp, cos_group, sin_group):
    first_child = grouped[:, 0]
    second_child = grouped[:, 1]
    results = []
    for target in range(2):
        summed = apply_matrix(first_child, interp[target, 0]) + apply_matrix(
            second_child, interp[target, 1]
        )
        results.append(rotate_phase(summed, cos_group[:, target], sin_group[:, target]))
    return jnp.stack(results, axis=1)


def partner_step(current, partner, upper_bit, interp, cosine, sine):
    mine_part = apply_matrix(current, interp[upper_bit, upper_bit])
    other_part = apply_matrix(partner, interp[upper_bit, 1 - upper_bit])
    return rotate_phase(mine_part + other_part, cosine, sine)


def general(weights, interp, slowness, box_coord):
    per_dev = weights.shape[0]
    rank_size = weights.shape[2]
    coords = box_coord.astype(jnp.float32)
    dist_angle = (
        coords[0][:, None] * slowness[0, 0][None, :] + coords[1][:, None] * slowness[0, 1][None, :]
    )
    local_angle = (
        coords[0][:, None] * slowness[1, 0][None, :] + coords[1][:, None] * slowness[1, 1][None, :]
    )
    dist_cos = jnp.cos(dist_angle)
    dist_sin = jnp.sin(dist_angle)
    local_cos = jnp.cos(local_angle)
    local_sin = jnp.sin(local_angle)
    current = weights
    for axis in ("bz", "by", "bx"):
        for bit_num in range(lax.axis_size(axis).bit_length() - 1):
            partner = from_partner(current, axis, bit_num)
            upper_bit = lax.axis_index(axis) >> bit_num & 1
            current = partner_step(current, partner, upper_bit, interp, dist_cos, dist_sin)
    for local_num in range(LOCAL):
        span_len = per_dev >> local_num + 1
        grouped = current.reshape(-1, 2, span_len, 2, rank_size)
        cos_group = local_cos.reshape(-1, 2, span_len, rank_size)
        sin_group = local_sin.reshape(-1, 2, span_len, rank_size)
        current = level_step(grouped, interp, cos_group, sin_group).reshape(per_dev, 2, rank_size)
    return current


def position():
    return lax.axis_index("bx") * lax.axis_size("by") + lax.axis_index("by")


def rows_of(value):
    return value.reshape(-1, value.shape[-1])


def swap_parts(tiles):
    row = lax.broadcasted_iota(jnp.int32, tiles.shape, 1)
    return jnp.where(
        row % 2 == 0, pltpu.roll(tiles, TILE - 1, axis=1), pltpu.roll(tiles, 1, axis=1)
    )


def rotate_tiles(summed, cosine, sine):
    return cosine * summed + sine * swap_parts(summed)


def even_rows(shape):
    return lax.broadcasted_iota(jnp.int32, shape, len(shape) - 2) % 2 == 0


def sin_cos(angle, flipped):
    quarter = jnp.floor(angle * 0.6366197723675814 + 0.5)
    rest = (angle - quarter * 1.5703125) - quarter * 4.838267948966e-4
    square = rest * rest
    odd_part = (-1.9515295891e-4 * square + 8.3321608736e-3) * square - 1.6666654611e-1
    odd_part = odd_part * (square * rest) + rest
    even_part = (2.443315711809948e-5 * square - 1.388731625493765e-3) * square
    even_part = ((even_part + 4.166664568298827e-2) * square - 0.5) * square + 1.0
    turn = quarter.astype(jnp.int32)
    odd = (turn & 1) != 0
    sine = jnp.where(odd, even_part, odd_part)
    cosine = jnp.where(odd, odd_part, even_part)
    return (
        jnp.where(((turn + flipped) & 2) != 0, -sine, sine),
        jnp.where(((turn + 1) & 2) != 0, -cosine, cosine),
    )


def paired_tables(coords, slow_x, slow_y, count):
    angle = jnp.stack(
        [
            coords[:, h : h + 1] * slow_x + coords[:, count + h : count + h + 1] * slow_y
            for h in range(count)
        ]
    )
    even = even_rows(angle.shape)
    sine, cosine = sin_cos(angle, jnp.where(even, 2, 0))
    return (
        jnp.where(even, cosine, pltpu.roll(cosine, 1, axis=1)),
        jnp.where(even, sine, -pltpu.roll(sine, 1, axis=1)),
        jnp.where(even, pltpu.roll(cosine, TILE - 1, axis=1), cosine),
        jnp.where(even, -pltpu.roll(sine, TILE - 1, axis=1), sine),
    )


def coord_kernel(count, highs, box_ref, coord_ref):
    slots = box_ref.shape[1]
    rank = coord_ref.shape[-1]
    low_count = slots // highs
    rows = count * TILE
    slot = lax.broadcasted_iota(jnp.int32, (rows, slots), 1)
    row = lax.broadcasted_iota(jnp.int32, (rows, slots), 0)
    mine = slot % low_count == row // (rows // low_count)
    high = lax.broadcasted_iota(jnp.int32, (slots, rank), 0) // low_count
    column = lax.broadcasted_iota(jnp.int32, (slots, rank), 1)
    coords = jnp.zeros((rows, rank), jnp.float32)
    for which in range(2):
        picked = jnp.where(mine, box_ref[which : which + 1].astype(jnp.float32), 0.0)
        fold = jnp.where(column == high + which * highs, 1.0, 0.0).astype(jnp.bfloat16)
        coords += jnp.dot(picked.astype(jnp.bfloat16), fold, preferred_element_type=jnp.float32)
    coord_ref[...] = coords.reshape(count, TILE, rank).astype(jnp.bfloat16)


def own_table_kernel(ks, highs, coord_ref, slow_ref, cos_ref, sin_ref):
    rank = coord_ref.shape[-1]
    slow_x = jnp.broadcast_to(slow_ref[0, 0:1], (TILE, rank))
    slow_y = jnp.broadcast_to(slow_ref[0, 1:2], (TILE, rank))
    for at in range(0, len(ks), 2):
        two = min(at + 1, len(ks) - 1)
        low, high = [
            coord_ref[jnp.bitwise_xor(position(), ks[one])].astype(jnp.float32) for one in (at, two)
        ]
        pair = jnp.where(even_rows(low.shape), low, high)
        tables = paired_tables(pair, slow_x, slow_y, highs)
        cos_ref[at], sin_ref[at] = tables[0], tables[1]
        if two != at:
            cos_ref[two], sin_ref[two] = tables[2], tables[3]


def owned(ref, count, highs, k):
    flat = ref.reshape(ref.shape[0] * ref.shape[1], ref.shape[2])
    to = jnp.bitwise_xor(position(), k)
    starts = [pl.multiple_of((h * count + to) * TILE, TILE) for h in range(highs)]
    return [flat[pl.ds(start, TILE), :] for start in starts]


def raw_kernel(ks, count, highs, own_ref, coord_ref, *out_refs):
    for out_ref, k in zip(out_refs, ks):
        for h, tile in enumerate(owned(own_ref, count, highs, k)):
            out_ref[h] = tile
        out_ref[highs] = coord_ref[jnp.bitwise_xor(position(), k)]


def table_kernel(highs, msg_ref, slow_ref, *out_refs):
    even = even_rows((TILE, slow_ref.shape[-1]))
    slow_x = jnp.where(even, slow_ref[0, 0:1], slow_ref[1, 0:1])
    slow_y = jnp.where(even, slow_ref[0, 1:2], slow_ref[1, 1:2])
    tables = paired_tables(msg_ref[highs].astype(jnp.float32), slow_x, slow_y, highs)
    for out_ref, table in zip(out_refs, tables):
        out_ref[...] = table


def mix(near, far, near_matrix, far_matrix):
    return jnp.dot(near, near_matrix, preferred_element_type=jnp.float32) + jnp.dot(
        far, far_matrix, preferred_element_type=jnp.float32
    )


def first_kernel(
    ks, count, highs, own_ref, other_ref, interp_ref, cos_ref, sin_ref, coord_ref, *out_refs
):
    upper = lax.axis_index("bz")
    rank = own_ref.shape[-1]
    blocks = [
        jnp.concatenate([tile for k in ks for tile in owned(ref, count, highs, k)])
        for ref in (own_ref, other_ref)
    ]
    summed = mix(*blocks, interp_ref[upper, upper], interp_ref[upper, 1 - upper])
    summed = summed.reshape(len(ks), highs, TILE, rank)
    for at, k in enumerate(ks):
        turned = rotate_tiles(summed[at], cos_ref[at], sin_ref[at])
        out_refs[at][0:highs] = turned.astype(jnp.bfloat16)
        out_refs[at][highs] = coord_ref[jnp.bitwise_xor(position(), k)]


def raised_kernel(size, highs, interp_ref, *rest):
    own_refs, other_refs, rest = rest[:size], rest[size : 2 * size], rest[2 * size :]
    table_refs, out_refs = rest[: 2 * size], rest[2 * size :]
    upper = lax.axis_index("bz")
    rank = interp_ref.shape[-1]
    own, other = [
        jnp.concatenate([rows_of(ref[0:highs].astype(jnp.float32)) for ref in refs])
        for refs in (own_refs, other_refs)
    ]
    summed = mix(
        own.astype(jnp.bfloat16),
        other.astype(jnp.bfloat16),
        interp_ref[upper, upper],
        interp_ref[upper, 1 - upper],
    ).reshape(size, highs, TILE, rank)
    for k in range(size):
        turned = rotate_tiles(summed[k], table_refs[2 * k][...], table_refs[2 * k + 1][...])
        out_refs[k][...] = turned.astype(jnp.bfloat16)


def device_level(children, upper, interp_ref):
    return [
        mix(children[t], children[1 - t], interp_ref[u, u], interp_ref[u, 1 - u])
        for t, u in ((0, upper), (1, 1 - upper))
    ]


def half_kernel(size, highs, interp_ref, *rest):
    msg_refs, table_refs, out_ref = rest[:size], rest[size : 3 * size], rest[3 * size]
    rank = interp_ref.shape[-1]
    bits = size.bit_length() - 1
    held = [rows_of(msg_refs[k][0:highs].astype(jnp.float32)).astype(jnp.bfloat16) for k in range(size)]
    for bit in range(bits):
        mine = jnp.right_shift(position(), bit) & 1
        groups = [[k for k in range(size) if k >> bit & 1 == t] for t in range(2)]
        children = [jnp.concatenate([held[k] for k in ks]) for ks in groups]
        for ks, summed in zip(groups, device_level(children, mine, interp_ref)):
            summed = summed.reshape(len(ks), highs, TILE, rank)
            for at, k in enumerate(ks):
                turned = rotate_tiles(summed[at], table_refs[2 * k][...], table_refs[2 * k + 1][...])
                if bit == bits - 1:
                    out_ref[k] = turned
                else:
                    held[k] = rows_of(turned).astype(jnp.bfloat16)


def final_kernel(places, highs, last_bit, flip, interp_ref, near_ref, other_ref, *rest):
    size = len(places)
    table_refs, out_refs, held = rest[: 4 * size], rest[4 * size : 5 * size], rest[5 * size]
    rank = interp_ref.shape[-1]
    upper = jnp.bitwise_xor(jnp.right_shift(position(), last_bit) & 1, flip)
    near, other = [
        jnp.concatenate([rows_of(ref[at]) for at in places]).astype(jnp.bfloat16)
        for ref in (near_ref, other_ref)
    ]
    summed = mix(near, other, interp_ref[upper, upper], interp_ref[upper, 1 - upper])
    summed = summed.reshape(size, highs, TILE, rank)
    for at in range(size):
        cos_ref, sin_ref = table_refs[4 * at : 4 * at + 2]
        held[at] = rotate_tiles(summed[at], cos_ref[...], sin_ref[...])
    for level in range(LOCAL):
        span = highs >> level + 1
        groups = [[h for h in range(highs) if (h // span) % 2 == t] for t in range(2)]
        children = []
        for t in range(2):
            tiles = [held[at, h] for at in range(size) for h in groups[t]]
            children.append(jnp.concatenate(tiles).astype(jnp.bfloat16))
        for t in range(2):
            summed = mix(children[0], children[1], interp_ref[t, 0], interp_ref[t, 1])
            summed = summed.reshape(size, highs // 2, TILE, rank)
            for at in range(size):
                cos_ref, sin_ref = table_refs[4 * at + 2 : 4 * at + 4]
                cosine = jnp.stack([cos_ref[h] for h in groups[t]])
                sine = jnp.stack([sin_ref[h] for h in groups[t]])
                turned = rotate_tiles(summed[at], cosine, sine)
                for place, h in enumerate(groups[t]):
                    if level == LOCAL - 1:
                        out_refs[at][h] = turned[place].astype(jnp.bfloat16)
                    else:
                        held[at, h] = turned[place]


def gather_kernel(count, highs, *rest):
    back_refs, (out_hbm, held, sems) = rest[:count], rest[count:]
    slots, parts, rank = held.shape
    flat = held.reshape(slots * parts, rank)
    pieces = sems.shape[0]
    copies = []
    for piece in range(pieces):
        for h in range(piece * highs // pieces, (piece + 1) * highs // pieces):
            for k in range(count):
                place = jnp.bitwise_xor(position(), k)
                start = pl.multiple_of((h * count + place) * TILE, TILE)
                flat[pl.ds(start, TILE), :] = back_refs[k][h]
        span = pl.ds(piece * slots // pieces, slots // pieces)
        copies.append(pltpu.make_async_copy(held.at[span], out_hbm.at[span], sems.at[piece]))
        copies[-1].start()
    for copy in copies:
        copy.wait()


def transposed(weights, interp, slowness, box_coord):
    per_dev, parts, rank = weights.shape
    count = lax.axis_size("bx") * lax.axis_size("by")
    half = count // 2
    highs = 1 << LOCAL
    bf16, f32 = jnp.bfloat16, jnp.float32
    vmem = pl.BlockSpec(memory_space=pltpu.VMEM)

    def call(kernel, in_specs, outs, scratch=(), flops=0, moved=0, room=12, place=vmem):
        return pl.pallas_call(
            kernel,
            in_specs=in_specs,
            out_specs=[place] * len(outs),
            out_shape=[jax.ShapeDtypeStruct(s, t) for s, t in outs],
            scratch_shapes=list(scratch),
            compiler_params=pltpu.CompilerParams(vmem_limit_bytes=room << 20),
            cost_estimate=pl.CostEstimate(flops=flops, bytes_accessed=moved, transcendentals=0),
        )

    def run(kernel, in_specs, outs, args, **options):
        return call(kernel, in_specs, outs, **options)(*args)

    def swap_with(block, axes, mask):
        size = 1
        for axis in axes:
            size *= lax.axis_size(axis)
        return lax.ppermute(block, axes, [(i, i ^ mask) for i in range(size)])

    other = swap_with(weights, ("bz",), 1)
    (coord,) = run(
        functools.partial(coord_kernel, count, highs),
        [vmem],
        [((count, TILE, rank), bf16)],
        (box_coord,),
        flops=1 << 31,
        moved=1 << 16,
        room=6,
    )
    messages = [None] * count
    raw = run(
        functools.partial(raw_kernel, RAW, count, highs),
        [vmem] * 2,
        [((highs + 1, TILE, rank), bf16)] * len(RAW),
        (weights, coord),
        flops=1 << 24,
        moved=1 << 19,
        room=6,
    )
    own_tables = run(
        functools.partial(own_table_kernel, MIXED, highs),
        [vmem] * 2,
        [((len(MIXED), highs, TILE, rank), f32)] * 2,
        (coord, slowness),
        flops=1 << 31,
        moved=1 << 20,
        room=6,
    )
    mixed = run(
        functools.partial(first_kernel, MIXED, count, highs),
        [vmem] * 6,
        [((highs + 1, TILE, rank), bf16)] * len(MIXED),
        (weights, other, interp, *own_tables, coord),
        flops=1 << 27,
        moved=1 << 20,
    )
    for ks, blocks in ((RAW, raw), (MIXED, mixed)):
        for k, block in zip(ks, blocks):
            messages[k] = block
    arrived = [messages[0]] + [swap_with(messages[k], ("bx", "by"), k) for k in range(1, count)]
    tables = [None] * count
    for k in range(count):
        tables[k] = run(
            functools.partial(table_kernel, highs),
            [vmem, vmem],
            [((highs, TILE, rank), f32)] * 4,
            (arrived[k], slowness),
            flops=1 << 22,
            moved=1 << 19,
            room=6,
        )
    tile_shape = (highs, TILE, rank)
    raised = run(
        functools.partial(raised_kernel, len(RAW), highs),
        [vmem] * (1 + 4 * len(RAW)),
        [(tile_shape, bf16)] * len(RAW),
        (
            interp,
            *[arrived[k] for k in RAW],
            *[swap_with(arrived[k], ("bz",), 1) for k in RAW],
            *[t for k in RAW for t in tables[k][:2]],
        ),
        flops=1 << 27,
        moved=1 << 20,
    )
    for k, block in zip(RAW, raised):
        arrived[k] = block
    halves = []
    for side in range(2):
        ks = range(side * half, side * half + half)
        (done,) = run(
            functools.partial(half_kernel, half, highs),
            [vmem] * (1 + 3 * half),
            [((half,) + tile_shape, f32)],
            (interp, *[arrived[k] for k in ks], *[t for k in ks for t in tables[k][:2]]),
            flops=1 << 29,
            moved=1 << 20,
        )
        halves.append(done)
    results = [None] * count
    for ks in FINALS.values():
        side, size = ks[0] // half, len(ks)
        outs = run(
            functools.partial(
                final_kernel, [k % half for k in ks], highs, count.bit_length() - 2, side
            ),
            [vmem] * (3 + 4 * size),
            [(tile_shape, bf16)] * size,
            (interp, halves[side], halves[1 - side], *[t for k in ks for t in tables[k]]),
            scratch=[pltpu.VMEM((size,) + tile_shape, f32)],
            flops=1 << 29,
            moved=1 << 20,
        )
        for k, out in zip(ks, outs):
            results[k] = out
    back = [results[0]] + [swap_with(results[k], ("bx", "by"), k) for k in range(1, count)]
    (gathered,) = run(
        functools.partial(gather_kernel, count, highs),
        [vmem] * count,
        [((per_dev, parts, rank), bf16)],
        tuple(back),
        scratch=[pltpu.VMEM((per_dev, parts, rank), bf16), pltpu.SemaphoreType.DMA((4,))],
        moved=1 << 20,
        place=pl.BlockSpec(memory_space=pl.ANY),
    )
    return gathered


def fits(mesh_shape):
    return mesh_shape["bx"] * mesh_shape["by"] == 8 and mesh_shape["bz"] == 2


def local(weights, interp, slowness, box_coord):
    sizes = {axis: lax.axis_size(axis) for axis in ("bx", "by", "bz")}
    if fits(sizes) and weights.shape[0] * weights.shape[1] == (TILE * 8) << LOCAL:
        return transposed(weights, interp, slowness, box_coord)
    return general(weights, interp, slowness, box_coord)


def solution(mesh):
    placed = (P(("shots", "bx", "by", "bz"), None, None), P(), P(), P(None, ("bx", "by", "bz")))
    return jax.shard_map(
        local,
        mesh=mesh,
        in_specs=placed,
        out_specs=P(("shots", "bx", "by", "bz"), None, None),
        check_vma=False,
    )
```

```python
import functools

import jax
import jax.numpy as jnp
from jax import lax
from jax.experimental import pallas as pl
from jax.experimental.pallas import tpu as pltpu
from jax.sharding import PartitionSpec as P


LOCAL = 4
TILE = 8
RAW = (4, 5, 6)
MIXED = (0, 1, 2, 3, 7)
FINALS = {"final_a": (4, 5, 6, 7), "final_c": (1, 2, 3), "final_d": (0,)}


def from_partner(block, axis, stride):
    count = lax.axis_size(axis)
    route = []
    for low in range(count):
        high = low | 1 << stride
        if high != low and high < count:
            route += [(low, high), (high, low)]
    return lax.ppermute(block, axis, route)


def apply_matrix(block, matrix):
    block_shape = block.shape
    product = jnp.dot(
        block.reshape(-1, block_shape[-1]), matrix, preferred_element_type=jnp.float32
    )
    return product.reshape(block_shape)


def rotate_phase(summed, cosine, sine):
    real_part = summed[..., 0, :]
    imag_part = summed[..., 1, :]
    return jnp.stack(
        [cosine * real_part - sine * imag_part, sine * real_part + cosine * imag_part], axis=-2
    ).astype(jnp.bfloat16)


def level_step(grouped, interp, cos_group, sin_group):
    first_child = grouped[:, 0]
    second_child = grouped[:, 1]
    results = []
    for target in range(2):
        summed = apply_matrix(first_child, interp[target, 0]) + apply_matrix(
            second_child, interp[target, 1]
        )
        results.append(rotate_phase(summed, cos_group[:, target], sin_group[:, target]))
    return jnp.stack(results, axis=1)


def partner_step(current, partner, upper_bit, interp, cosine, sine):
    mine_part = apply_matrix(current, interp[upper_bit, upper_bit])
    other_part = apply_matrix(partner, interp[upper_bit, 1 - upper_bit])
    return rotate_phase(mine_part + other_part, cosine, sine)


def general(weights, interp, slowness, box_coord):
    per_dev = weights.shape[0]
    rank_size = weights.shape[2]
    coords = box_coord.astype(jnp.float32)
    dist_angle = (
        coords[0][:, None] * slowness[0, 0][None, :] + coords[1][:, None] * slowness[0, 1][None, :]
    )
    local_angle = (
        coords[0][:, None] * slowness[1, 0][None, :] + coords[1][:, None] * slowness[1, 1][None, :]
    )
    dist_cos = jnp.cos(dist_angle)
    dist_sin = jnp.sin(dist_angle)
    local_cos = jnp.cos(local_angle)
    local_sin = jnp.sin(local_angle)
    current = weights
    for axis in ("bz", "by", "bx"):
        for bit_num in range(lax.axis_size(axis).bit_length() - 1):
            partner = from_partner(current, axis, bit_num)
            upper_bit = lax.axis_index(axis) >> bit_num & 1
            current = partner_step(current, partner, upper_bit, interp, dist_cos, dist_sin)
    for local_num in range(LOCAL):
        span_len = per_dev >> local_num + 1
        grouped = current.reshape(-1, 2, span_len, 2, rank_size)
        cos_group = local_cos.reshape(-1, 2, span_len, rank_size)
        sin_group = local_sin.reshape(-1, 2, span_len, rank_size)
        current = level_step(grouped, interp, cos_group, sin_group).reshape(per_dev, 2, rank_size)
    return current


def position():
    return lax.axis_index("bx") * lax.axis_size("by") + lax.axis_index("by")


def rows_of(value):
    return value.reshape(-1, value.shape[-1])


def pick_rows(tiles, rows_from):
    source = rows_from(lax.broadcasted_iota(jnp.int32, tiles.shape[1:], 0))
    return jnp.stack(
        [jnp.take_along_axis(tiles[at], source, axis=0) for at in range(tiles.shape[0])]
    )


def swap_parts(tiles):
    return pick_rows(tiles, lambda row: jnp.bitwise_xor(row, 1))


def rotate_tiles(summed, cosine, sine):
    return cosine * summed + sine * swap_parts(summed)


def even_rows(shape):
    return lax.broadcasted_iota(jnp.int32, shape, len(shape) - 2) % 2 == 0


def sin_cos(angle, flipped):
    quarter = jnp.floor(angle * 0.6366197723675814 + 0.5)
    rest = (angle - quarter * 1.5703125) - quarter * 4.838267948966e-4
    square = rest * rest
    odd_part = (-1.9515295891e-4 * square + 8.3321608736e-3) * square - 1.6666654611e-1
    odd_part = odd_part * (square * rest) + rest
    even_part = (2.443315711809948e-5 * square - 1.388731625493765e-3) * square
    even_part = ((even_part + 4.166664568298827e-2) * square - 0.5) * square + 1.0
    turn = quarter.astype(jnp.int32)
    odd = (turn & 1) != 0
    sine = jnp.where(odd, even_part, odd_part)
    cosine = jnp.where(odd, odd_part, even_part)
    return (
        jnp.where(((turn + flipped) & 2) != 0, -sine, sine),
        jnp.where(((turn + 1) & 2) != 0, -cosine, cosine),
    )


def paired_tables(coords, slow_x, slow_y, count):
    angle = jnp.stack(
        [
            coords[:, h : h + 1] * slow_x + coords[:, count + h : count + h + 1] * slow_y
            for h in range(count)
        ]
    )
    sine, cosine = sin_cos(angle, jnp.where(even_rows(angle.shape), 2, 0))
    sign = jnp.where(even_rows(angle.shape), 1.0, -1.0)

    def even_row(row):
        return row - row % 2

    def odd_row(row):
        return row - row % 2 + 1

    return (
        pick_rows(cosine, even_row),
        pick_rows(sine, even_row) * sign,
        pick_rows(cosine, odd_row),
        pick_rows(sine, odd_row) * -sign,
    )


def coord_kernel(count, highs, box_ref, coord_ref):
    slots = box_ref.shape[1]
    rank = coord_ref.shape[-1]
    low_count = slots // highs
    rows = count * TILE
    slot = lax.broadcasted_iota(jnp.int32, (rows, slots), 1)
    row = lax.broadcasted_iota(jnp.int32, (rows, slots), 0)
    mine = slot % low_count == row // (rows // low_count)
    high = lax.broadcasted_iota(jnp.int32, (slots, rank), 0) // low_count
    column = lax.broadcasted_iota(jnp.int32, (slots, rank), 1)
    coords = jnp.zeros((rows, rank), jnp.float32)
    for which in range(2):
        picked = jnp.where(mine, box_ref[which : which + 1].astype(jnp.float32), 0.0)
        fold = jnp.where(column == high + which * highs, 1.0, 0.0).astype(jnp.bfloat16)
        coords += jnp.dot(picked.astype(jnp.bfloat16), fold, preferred_element_type=jnp.float32)
    coord_ref[...] = coords.reshape(count, TILE, rank).astype(jnp.bfloat16)


def mixed_slopes(slow_ref):
    even = even_rows((TILE, slow_ref.shape[-1]))
    return [jnp.where(even, slow_ref[0, at : at + 1], slow_ref[1, at : at + 1]) for at in range(2)]


def own_table_kernel(ks, highs, coord_ref, slow_ref, cos_ref, sin_ref, *own_refs):
    rank = coord_ref.shape[-1]
    slow_x = jnp.broadcast_to(slow_ref[0, 0:1], (TILE, rank))
    slow_y = jnp.broadcast_to(slow_ref[0, 1:2], (TILE, rank))

    def coords(k):
        return coord_ref[jnp.bitwise_xor(position(), k)].astype(jnp.float32)

    for out_ref, table in zip(own_refs, paired_tables(coords(0), *mixed_slopes(slow_ref), highs)):
        out_ref[...] = table
    for at in range(0, len(ks), 2):
        two = min(at + 1, len(ks) - 1)
        low, high = coords(ks[at]), coords(ks[two])
        pair = jnp.where(even_rows(low.shape), low, high)
        tables = paired_tables(pair, slow_x, slow_y, highs)
        cos_ref[at], sin_ref[at] = tables[0], tables[1]
        if two != at:
            cos_ref[two], sin_ref[two] = tables[2], tables[3]


def owned(ref, count, highs, k):
    flat = ref.reshape(ref.shape[0] * ref.shape[1], ref.shape[2])
    to = jnp.bitwise_xor(position(), k)
    starts = [pl.multiple_of((h * count + to) * TILE, TILE) for h in range(highs)]
    return [flat[pl.ds(start, TILE), :] for start in starts]


def raw_kernel(ks, count, highs, own_ref, coord_ref, *out_refs):
    for out_ref, k in zip(out_refs, ks):
        for h, tile in enumerate(owned(own_ref, count, highs, k)):
            out_ref[h] = tile
        out_ref[highs] = coord_ref[jnp.bitwise_xor(position(), k)]


def table_kernel(highs, msg_ref, slow_ref, *out_refs):
    coords = msg_ref[highs].astype(jnp.float32)
    for out_ref, table in zip(out_refs, paired_tables(coords, *mixed_slopes(slow_ref), highs)):
        out_ref[...] = table


def mix(near, far, near_matrix, far_matrix):
    return jnp.dot(near, near_matrix, preferred_element_type=jnp.float32) + jnp.dot(
        far, far_matrix, preferred_element_type=jnp.float32
    )


def first_kernel(ks, count, highs, own_ref, other_ref, interp_ref, coord_ref, *rest):
    cos_ref, sin_ref, here_cos_ref, here_sin_ref = rest[:4]
    out_refs = rest[4:]
    upper = lax.axis_index("bz")
    rank = own_ref.shape[-1]
    blocks = [
        jnp.concatenate([tile for k in ks for tile in owned(ref, count, highs, k)])
        for ref in (own_ref, other_ref)
    ]
    summed = mix(*blocks, interp_ref[upper, upper], interp_ref[upper, 1 - upper])
    summed = summed.reshape(len(ks), highs, TILE, rank)
    for at, k in enumerate(ks):
        tables = (here_cos_ref[...], here_sin_ref[...]) if k == 0 else (cos_ref[at - 1], sin_ref[at - 1])
        turned = rotate_tiles(summed[at], *tables)
        out_refs[at][0:highs] = turned.astype(jnp.bfloat16)
        out_refs[at][highs] = coord_ref[jnp.bitwise_xor(position(), k)]


def raised_kernel(size, highs, interp_ref, *rest):
    own_refs, other_refs, rest = rest[:size], rest[size : 2 * size], rest[2 * size :]
    table_refs, out_refs = rest[: 2 * size], rest[2 * size :]
    upper = lax.axis_index("bz")
    rank = interp_ref.shape[-1]
    own, other = [
        jnp.concatenate([rows_of(ref[0:highs].astype(jnp.float32)) for ref in refs])
        for refs in (own_refs, other_refs)
    ]
    summed = mix(
        own.astype(jnp.bfloat16),
        other.astype(jnp.bfloat16),
        interp_ref[upper, upper],
        interp_ref[upper, 1 - upper],
    ).reshape(size, highs, TILE, rank)
    for k in range(size):
        turned = rotate_tiles(summed[k], table_refs[2 * k][...], table_refs[2 * k + 1][...])
        out_refs[k][...] = turned.astype(jnp.bfloat16)


def device_level(children, upper, interp_ref):
    return [
        mix(children[t], children[1 - t], interp_ref[u, u], interp_ref[u, 1 - u])
        for t, u in ((0, upper), (1, 1 - upper))
    ]


def half_kernel(size, highs, interp_ref, *rest):
    msg_refs, table_refs, out_ref = rest[:size], rest[size : 3 * size], rest[3 * size]
    rank = interp_ref.shape[-1]
    bits = size.bit_length() - 1
    held = [rows_of(msg_refs[k][0:highs].astype(jnp.float32)).astype(jnp.bfloat16) for k in range(size)]
    for bit in range(bits):
        mine = jnp.right_shift(position(), bit) & 1
        groups = [[k for k in range(size) if k >> bit & 1 == t] for t in range(2)]
        children = [jnp.concatenate([held[k] for k in ks]) for ks in groups]
        for ks, summed in zip(groups, device_level(children, mine, interp_ref)):
            summed = summed.reshape(len(ks), highs, TILE, rank)
            for at, k in enumerate(ks):
                turned = rotate_tiles(summed[at], table_refs[2 * k][...], table_refs[2 * k + 1][...])
                if bit == bits - 1:
                    out_ref[k] = turned
                else:
                    held[k] = rows_of(turned).astype(jnp.bfloat16)


def final_kernel(places, highs, last_bit, flip, interp_ref, near_ref, other_ref, *rest):
    size = len(places)
    table_refs, out_refs, held = rest[: 4 * size], rest[4 * size : 5 * size], rest[5 * size]
    rank = interp_ref.shape[-1]
    upper = jnp.bitwise_xor(jnp.right_shift(position(), last_bit) & 1, flip)
    near, other = [
        jnp.concatenate([rows_of(ref[at]) for at in places]).astype(jnp.bfloat16)
        for ref in (near_ref, other_ref)
    ]
    summed = mix(near, other, interp_ref[upper, upper], interp_ref[upper, 1 - upper])
    summed = summed.reshape(size, highs, TILE, rank)
    for at in range(size):
        cos_ref, sin_ref = table_refs[4 * at : 4 * at + 2]
        held[at] = rotate_tiles(summed[at], cos_ref[...], sin_ref[...])
    for level in range(LOCAL):
        span = highs >> level + 1
        groups = [[h for h in range(highs) if (h // span) % 2 == t] for t in range(2)]
        children = []
        for t in range(2):
            tiles = [held[at, h] for at in range(size) for h in groups[t]]
            children.append(jnp.concatenate(tiles).astype(jnp.bfloat16))
        for t in range(2):
            summed = mix(children[0], children[1], interp_ref[t, 0], interp_ref[t, 1])
            summed = summed.reshape(size, highs // 2, TILE, rank)
            for at in range(size):
                cos_ref, sin_ref = table_refs[4 * at + 2 : 4 * at + 4]
                cosine = jnp.stack([cos_ref[h] for h in groups[t]])
                sine = jnp.stack([sin_ref[h] for h in groups[t]])
                turned = rotate_tiles(summed[at], cosine, sine)
                for place, h in enumerate(groups[t]):
                    if level == LOCAL - 1:
                        out_refs[at][h] = turned[place].astype(jnp.bfloat16)
                    else:
                        held[at, h] = turned[place]


def gather_kernel(count, highs, *rest):
    back_refs, (out_hbm, held, sems) = rest[:count], rest[count:]
    slots, parts, rank = held.shape
    flat = held.reshape(slots * parts, rank)
    pieces = sems.shape[0]
    copies = []
    for piece in range(pieces):
        for h in range(piece * highs // pieces, (piece + 1) * highs // pieces):
            for k in range(count):
                place = jnp.bitwise_xor(position(), k)
                start = pl.multiple_of((h * count + place) * TILE, TILE)
                flat[pl.ds(start, TILE), :] = back_refs[k][h]
        span = pl.ds(piece * slots // pieces, slots // pieces)
        copies.append(pltpu.make_async_copy(held.at[span], out_hbm.at[span], sems.at[piece]))
        copies[-1].start()
    for copy in copies:
        copy.wait()


def transposed(weights, interp, slowness, box_coord):
    per_dev, parts, rank = weights.shape
    count = lax.axis_size("bx") * lax.axis_size("by")
    half = count // 2
    highs = 1 << LOCAL
    bf16, f32 = jnp.bfloat16, jnp.float32
    vmem = pl.BlockSpec(memory_space=pltpu.VMEM)

    def call(kernel, in_specs, outs, scratch=(), flops=0, moved=0, room=12, place=vmem):
        return pl.pallas_call(
            kernel,
            in_specs=in_specs,
            out_specs=[place] * len(outs),
            out_shape=[jax.ShapeDtypeStruct(s, t) for s, t in outs],
            scratch_shapes=list(scratch),
            compiler_params=pltpu.CompilerParams(vmem_limit_bytes=room << 20),
            cost_estimate=pl.CostEstimate(flops=flops, bytes_accessed=moved, transcendentals=0),
        )

    def run(kernel, in_specs, outs, args, **options):
        return call(kernel, in_specs, outs, **options)(*args)

    def swap_with(block, axes, mask):
        size = 1
        for axis in axes:
            size *= lax.axis_size(axis)
        return lax.ppermute(block, axes, [(i, i ^ mask) for i in range(size)])

    other = swap_with(weights, ("bz",), 1)
    (coord,) = run(
        functools.partial(coord_kernel, count, highs),
        [vmem],
        [((count, TILE, rank), bf16)],
        (box_coord,),
        flops=1 << 31,
        moved=1 << 16,
        room=6,
    )
    messages = [None] * count
    raw = run(
        functools.partial(raw_kernel, RAW, count, highs),
        [vmem] * 2,
        [((highs + 1, TILE, rank), bf16)] * len(RAW),
        (weights, coord),
        flops=1 << 24,
        moved=1 << 19,
        room=6,
    )
    others = len(MIXED) - 1
    tile_shape = (highs, TILE, rank)
    own_cos, own_sin, *here = run(
        functools.partial(own_table_kernel, MIXED[1:], highs),
        [vmem] * 2,
        [((others,) + tile_shape, f32)] * 2 + [(tile_shape, f32)] * 4,
        (coord, slowness),
        flops=1 << 31,
        moved=1 << 20,
        room=6,
    )
    mixed = run(
        functools.partial(first_kernel, MIXED, count, highs),
        [vmem] * 8,
        [((highs + 1, TILE, rank), bf16)] * len(MIXED),
        (weights, other, interp, coord, own_cos, own_sin, *here[:2]),
        flops=1 << 27,
        moved=1 << 20,
    )
    for ks, blocks in ((RAW, raw), (MIXED, mixed)):
        for k, block in zip(ks, blocks):
            messages[k] = block
    arrived = [messages[0]] + [swap_with(messages[k], ("bx", "by"), k) for k in range(1, count)]
    tables = [here] + [None] * (count - 1)
    for k in range(1, count):
        tables[k] = run(
            functools.partial(table_kernel, highs),
            [vmem, vmem],
            [((highs, TILE, rank), f32)] * 4,
            (arrived[k], slowness),
            flops=1 << 22,
            moved=1 << 19,
            room=6,
        )
    raised = run(
        functools.partial(raised_kernel, len(RAW), highs),
        [vmem] * (1 + 4 * len(RAW)),
        [(tile_shape, bf16)] * len(RAW),
        (
            interp,
            *[arrived[k] for k in RAW],
            *[swap_with(arrived[k], ("bz",), 1) for k in RAW],
            *[t for k in RAW for t in tables[k][:2]],
        ),
        flops=1 << 27,
        moved=1 << 20,
    )
    for k, block in zip(RAW, raised):
        arrived[k] = block
    halves = []
    for side in range(2):
        ks = range(side * half, side * half + half)
        (done,) = run(
            functools.partial(half_kernel, half, highs),
            [vmem] * (1 + 3 * half),
            [((half,) + tile_shape, f32)],
            (interp, *[arrived[k] for k in ks], *[t for k in ks for t in tables[k][:2]]),
            flops=1 << 29,
            moved=1 << 20,
        )
        halves.append(done)
    results = [None] * count
    for ks in FINALS.values():
        side, size = ks[0] // half, len(ks)
        outs = run(
            functools.partial(
                final_kernel, [k % half for k in ks], highs, count.bit_length() - 2, side
            ),
            [vmem] * (3 + 4 * size),
            [(tile_shape, bf16)] * size,
            (interp, halves[side], halves[1 - side], *[t for k in ks for t in tables[k]]),
            scratch=[pltpu.VMEM((size,) + tile_shape, f32)],
            flops=1 << 29,
            moved=1 << 20,
        )
        for k, out in zip(ks, outs):
            results[k] = out
    back = [results[0]] + [swap_with(results[k], ("bx", "by"), k) for k in range(1, count)]
    (gathered,) = run(
        functools.partial(gather_kernel, count, highs),
        [vmem] * count,
        [((per_dev, parts, rank), bf16)],
        tuple(back),
        scratch=[pltpu.VMEM((per_dev, parts, rank), bf16), pltpu.SemaphoreType.DMA((4,))],
        moved=1 << 20,
        place=pl.BlockSpec(memory_space=pl.ANY),
    )
    return gathered


def fits(mesh_shape):
    return mesh_shape["bx"] * mesh_shape["by"] == 8 and mesh_shape["bz"] == 2


def local(weights, interp, slowness, box_coord):
    sizes = {axis: lax.axis_size(axis) for axis in ("bx", "by", "bz")}
    if fits(sizes) and weights.shape[0] * weights.shape[1] == (TILE * 8) << LOCAL:
        return transposed(weights, interp, slowness, box_coord)
    return general(weights, interp, slowness, box_coord)


def solution(mesh):
    placed = (P(("shots", "bx", "by", "bz"), None, None), P(), P(), P(None, ("bx", "by", "bz")))
    return jax.shard_map(
        local,
        mesh=mesh,
        in_specs=placed,
        out_specs=P(("shots", "bx", "by", "bz"), None, None),
        check_vma=False,
    )
```

```python
import functools

import jax
import jax.numpy as jnp
from jax import lax
from jax.experimental import pallas as pl
from jax.experimental.pallas import tpu as pltpu
from jax.sharding import PartitionSpec as P


LOCAL = 4
TILE = 8
RAW = (4, 5, 6)
MIXED = (0, 1, 2, 3, 7)
FINALS = {"final_a": (4, 5, 6, 7), "final_c": (1, 2, 3), "final_d": (0,)}
TABLES = ((4,), (5,), (6,), (2, 3), (1,), (7,))
LAST = (4, 3, 2, 1)


def from_partner(block, axis, stride):
    count = lax.axis_size(axis)
    route = []
    for low in range(count):
        high = low | 1 << stride
        if high != low and high < count:
            route += [(low, high), (high, low)]
    return lax.ppermute(block, axis, route)


def apply_matrix(block, matrix):
    block_shape = block.shape
    product = jnp.dot(
        block.reshape(-1, block_shape[-1]), matrix, preferred_element_type=jnp.float32
    )
    return product.reshape(block_shape)


def rotate_phase(summed, cosine, sine):
    real_part = summed[..., 0, :]
    imag_part = summed[..., 1, :]
    return jnp.stack(
        [cosine * real_part - sine * imag_part, sine * real_part + cosine * imag_part], axis=-2
    ).astype(jnp.bfloat16)


def level_step(grouped, interp, cos_group, sin_group):
    first_child = grouped[:, 0]
    second_child = grouped[:, 1]
    results = []
    for target in range(2):
        summed = apply_matrix(first_child, interp[target, 0]) + apply_matrix(
            second_child, interp[target, 1]
        )
        results.append(rotate_phase(summed, cos_group[:, target], sin_group[:, target]))
    return jnp.stack(results, axis=1)


def partner_step(current, partner, upper_bit, interp, cosine, sine):
    mine_part = apply_matrix(current, interp[upper_bit, upper_bit])
    other_part = apply_matrix(partner, interp[upper_bit, 1 - upper_bit])
    return rotate_phase(mine_part + other_part, cosine, sine)


def general(weights, interp, slowness, box_coord):
    per_dev = weights.shape[0]
    rank_size = weights.shape[2]
    coords = box_coord.astype(jnp.float32)
    dist_angle = (
        coords[0][:, None] * slowness[0, 0][None, :] + coords[1][:, None] * slowness[0, 1][None, :]
    )
    local_angle = (
        coords[0][:, None] * slowness[1, 0][None, :] + coords[1][:, None] * slowness[1, 1][None, :]
    )
    dist_cos = jnp.cos(dist_angle)
    dist_sin = jnp.sin(dist_angle)
    local_cos = jnp.cos(local_angle)
    local_sin = jnp.sin(local_angle)
    current = weights
    for axis in ("bz", "by", "bx"):
        for bit_num in range(lax.axis_size(axis).bit_length() - 1):
            partner = from_partner(current, axis, bit_num)
            upper_bit = lax.axis_index(axis) >> bit_num & 1
            current = partner_step(current, partner, upper_bit, interp, dist_cos, dist_sin)
    for local_num in range(LOCAL):
        span_len = per_dev >> local_num + 1
        grouped = current.reshape(-1, 2, span_len, 2, rank_size)
        cos_group = local_cos.reshape(-1, 2, span_len, rank_size)
        sin_group = local_sin.reshape(-1, 2, span_len, rank_size)
        current = level_step(grouped, interp, cos_group, sin_group).reshape(per_dev, 2, rank_size)
    return current


def position():
    return lax.axis_index("bx") * lax.axis_size("by") + lax.axis_index("by")


def rows_of(value):
    return value.reshape(-1, value.shape[-1])


def pick_rows(tiles, rows_from):
    source = rows_from(lax.broadcasted_iota(jnp.int32, tiles.shape[1:], 0))
    return jnp.stack(
        [jnp.take_along_axis(tiles[at], source, axis=0) for at in range(tiles.shape[0])]
    )


def swap_parts(tiles):
    return pick_rows(tiles, lambda row: jnp.bitwise_xor(row, 1))


def rotate_tiles(summed, cosine, sine):
    return cosine * summed + sine * swap_parts(summed)


def even_rows(shape):
    return lax.broadcasted_iota(jnp.int32, shape, len(shape) - 2) % 2 == 0


def sin_cos(angle, flipped):
    quarter = jnp.floor(angle * 0.6366197723675814 + 0.5)
    rest = (angle - quarter * 1.5703125) - quarter * 4.838267948966e-4
    square = rest * rest
    odd_part = (-1.9515295891e-4 * square + 8.3321608736e-3) * square - 1.6666654611e-1
    odd_part = odd_part * (square * rest) + rest
    even_part = (2.443315711809948e-5 * square - 1.388731625493765e-3) * square
    even_part = ((even_part + 4.166664568298827e-2) * square - 0.5) * square + 1.0
    turn = quarter.astype(jnp.int32)
    odd = (turn & 1) != 0
    sine = jnp.where(odd, even_part, odd_part)
    cosine = jnp.where(odd, odd_part, even_part)
    return (
        jnp.where(((turn + flipped) & 2) != 0, -sine, sine),
        jnp.where(((turn + 1) & 2) != 0, -cosine, cosine),
    )


def paired_tables(coords, slow_x, slow_y, count):
    angle = jnp.stack(
        [
            coords[:, h : h + 1] * slow_x + coords[:, count + h : count + h + 1] * slow_y
            for h in range(count)
        ]
    )
    sine, cosine = sin_cos(angle, jnp.where(even_rows(angle.shape), 2, 0))
    sign = jnp.where(even_rows(angle.shape), 1.0, -1.0)

    def even_row(row):
        return row - row % 2

    def odd_row(row):
        return row - row % 2 + 1

    return (
        pick_rows(cosine, even_row),
        pick_rows(sine, even_row) * sign,
        pick_rows(cosine, odd_row),
        pick_rows(sine, odd_row) * -sign,
    )


def coord_kernel(count, highs, box_ref, coord_ref):
    slots = box_ref.shape[1]
    rank = coord_ref.shape[-1]
    wide = 128
    low_count = slots // highs
    rows = count * TILE
    slot = lax.broadcasted_iota(jnp.int32, (rows, slots), 1)
    row = lax.broadcasted_iota(jnp.int32, (rows, slots), 0)
    mine = slot % low_count == row // (rows // low_count)
    high = lax.broadcasted_iota(jnp.int32, (slots, wide), 0) // low_count
    column = lax.broadcasted_iota(jnp.int32, (slots, wide), 1)
    coords = jnp.zeros((rows, wide), jnp.float32)
    for which in range(2):
        picked = jnp.where(mine, box_ref[which : which + 1].astype(jnp.float32), 0.0)
        fold = jnp.where(column == high + which * highs, 1.0, 0.0).astype(jnp.bfloat16)
        coords += jnp.dot(picked.astype(jnp.bfloat16), fold, preferred_element_type=jnp.float32)
    coord_ref[:, :, 0:wide] = coords.reshape(count, TILE, wide).astype(jnp.bfloat16)
    coord_ref[:, :, wide:rank] = jnp.zeros((count, TILE, rank - wide), jnp.bfloat16)


def mixed_slopes(slow_ref):
    even = even_rows((TILE, slow_ref.shape[-1]))
    return [jnp.where(even, slow_ref[0, at : at + 1], slow_ref[1, at : at + 1]) for at in range(2)]


def own_table_kernel(ks, highs, coord_ref, slow_ref, cos_ref, sin_ref, *own_refs):
    rank = coord_ref.shape[-1]
    slow_x = jnp.broadcast_to(slow_ref[0, 0:1], (TILE, rank))
    slow_y = jnp.broadcast_to(slow_ref[0, 1:2], (TILE, rank))

    def coords(k):
        return coord_ref[jnp.bitwise_xor(position(), k)].astype(jnp.float32)

    for out_ref, table in zip(own_refs, paired_tables(coords(0), *mixed_slopes(slow_ref), highs)):
        out_ref[...] = table
    for at in range(0, len(ks), 2):
        two = min(at + 1, len(ks) - 1)
        low, high = coords(ks[at]), coords(ks[two])
        pair = jnp.where(even_rows(low.shape), low, high)
        tables = paired_tables(pair, slow_x, slow_y, highs)
        cos_ref[at], sin_ref[at] = tables[0], tables[1]
        if two != at:
            cos_ref[two], sin_ref[two] = tables[2], tables[3]


def owned(ref, count, highs, k):
    flat = ref.reshape(ref.shape[0] * ref.shape[1], ref.shape[2])
    to = jnp.bitwise_xor(position(), k)
    starts = [pl.multiple_of((h * count + to) * TILE, TILE) for h in range(highs)]
    return [flat[pl.ds(start, TILE), :] for start in starts]


def raw_kernel(ks, count, highs, own_ref, coord_ref, *out_refs):
    for out_ref, k in zip(out_refs, ks):
        for h, tile in enumerate(owned(own_ref, count, highs, k)):
            out_ref[h] = tile
        out_ref[highs] = coord_ref[jnp.bitwise_xor(position(), k)]


def table_kernel(size, highs, *rest):
    msg_refs, slow_ref, out_refs = rest[:size], rest[size], rest[size + 1 :]
    for at, msg_ref in enumerate(msg_refs):
        coords = msg_ref[highs].astype(jnp.float32)
        tables = paired_tables(coords, *mixed_slopes(slow_ref), highs)
        for out_ref, table in zip(out_refs[4 * at : 4 * at + 4], tables):
            out_ref[...] = table


def mix(near, far, near_matrix, far_matrix):
    return jnp.dot(near, near_matrix, preferred_element_type=jnp.float32) + jnp.dot(
        far, far_matrix, preferred_element_type=jnp.float32
    )


def first_kernel(ks, count, highs, own_ref, other_ref, interp_ref, coord_ref, *rest):
    cos_ref, sin_ref, here_cos_ref, here_sin_ref = rest[:4]
    out_refs = rest[4:]
    upper = lax.axis_index("bz")
    rank = own_ref.shape[-1]
    blocks = [
        jnp.concatenate([tile for k in ks for tile in owned(ref, count, highs, k)])
        for ref in (own_ref, other_ref)
    ]
    summed = mix(*blocks, interp_ref[upper, upper], interp_ref[upper, 1 - upper])
    summed = summed.reshape(len(ks), highs, TILE, rank)
    for at, k in enumerate(ks):
        tables = (here_cos_ref[...], here_sin_ref[...]) if k == 0 else (cos_ref[at - 1], sin_ref[at - 1])
        turned = rotate_tiles(summed[at], *tables)
        out_refs[at][0:highs] = turned.astype(jnp.bfloat16)
        out_refs[at][highs] = coord_ref[jnp.bitwise_xor(position(), k)]


def raised_kernel(size, highs, interp_ref, *rest):
    own_refs, other_refs, rest = rest[:size], rest[size : 2 * size], rest[2 * size :]
    table_refs, out_refs = rest[: 2 * size], rest[2 * size :]
    upper = lax.axis_index("bz")
    rank = interp_ref.shape[-1]
    own, other = [
        jnp.concatenate([rows_of(ref[0:highs].astype(jnp.float32)) for ref in refs])
        for refs in (own_refs, other_refs)
    ]
    summed = mix(
        own.astype(jnp.bfloat16),
        other.astype(jnp.bfloat16),
        interp_ref[upper, upper],
        interp_ref[upper, 1 - upper],
    ).reshape(size, highs, TILE, rank)
    for k in range(size):
        turned = rotate_tiles(summed[k], table_refs[2 * k][...], table_refs[2 * k + 1][...])
        out_refs[k][...] = turned.astype(jnp.bfloat16)


def device_level(children, upper, interp_ref):
    return [
        mix(children[t], children[1 - t], interp_ref[u, u], interp_ref[u, 1 - u])
        for t, u in ((0, upper), (1, 1 - upper))
    ]


def half_kernel(size, highs, interp_ref, *rest):
    msg_refs, table_refs, out_ref = rest[:size], rest[size : 3 * size], rest[3 * size]
    rank = interp_ref.shape[-1]
    bits = size.bit_length() - 1
    held = [rows_of(msg_refs[k][0:highs].astype(jnp.float32)).astype(jnp.bfloat16) for k in range(size)]
    for bit in range(bits):
        mine = jnp.right_shift(position(), bit) & 1
        groups = [[k for k in range(size) if k >> bit & 1 == t] for t in range(2)]
        children = [jnp.concatenate([held[k] for k in ks]) for ks in groups]
        for ks, summed in zip(groups, device_level(children, mine, interp_ref)):
            summed = summed.reshape(len(ks), highs, TILE, rank)
            for at, k in enumerate(ks):
                turned = rotate_tiles(summed[at], table_refs[2 * k][...], table_refs[2 * k + 1][...])
                if bit == bits - 1:
                    out_ref[k] = turned
                else:
                    held[k] = rows_of(turned).astype(jnp.bfloat16)


def final_kernel(places, highs, last_bit, flip, interp_ref, near_ref, other_ref, *rest):
    size = len(places)
    table_refs, out_refs, held = rest[: 4 * size], rest[4 * size : 5 * size], rest[5 * size]
    rank = interp_ref.shape[-1]
    upper = jnp.bitwise_xor(jnp.right_shift(position(), last_bit) & 1, flip)
    near, other = [
        jnp.concatenate([rows_of(ref[at]) for at in places]).astype(jnp.bfloat16)
        for ref in (near_ref, other_ref)
    ]
    summed = mix(near, other, interp_ref[upper, upper], interp_ref[upper, 1 - upper])
    summed = summed.reshape(size, highs, TILE, rank)
    for at in range(size):
        cos_ref, sin_ref = table_refs[4 * at : 4 * at + 2]
        held[at] = rotate_tiles(summed[at], cos_ref[...], sin_ref[...])
    for level in range(LOCAL):
        span = highs >> level + 1
        groups = [[h for h in range(highs) if (h // span) % 2 == t] for t in range(2)]
        children = []
        for t in range(2):
            tiles = [held[at, h] for at in range(size) for h in groups[t]]
            children.append(jnp.concatenate(tiles).astype(jnp.bfloat16))
        for t in range(2):
            summed = mix(children[0], children[1], interp_ref[t, 0], interp_ref[t, 1])
            summed = summed.reshape(size, highs // 2, TILE, rank)
            for at in range(size):
                cos_ref, sin_ref = table_refs[4 * at + 2 : 4 * at + 4]
                cosine = jnp.stack([cos_ref[h] for h in groups[t]])
                sine = jnp.stack([sin_ref[h] for h in groups[t]])
                turned = rotate_tiles(summed[at], cosine, sine)
                for place, h in enumerate(groups[t]):
                    if level == LOCAL - 1:
                        out_refs[at][h] = turned[place].astype(jnp.bfloat16)
                    else:
                        held[at, h] = turned[place]


def gather_kernel(ks, count, highs, *rest):
    back_refs, (out_hbm, held, sems) = rest[: len(ks)], rest[len(ks) :]
    slots, parts, rank = held.shape
    flat = held.reshape(slots * parts, rank)
    pieces = sems.shape[0]
    copies = []
    for piece in range(pieces):
        for h in range(piece * highs // pieces, (piece + 1) * highs // pieces):
            for back_ref, k in zip(back_refs, ks):
                place = jnp.bitwise_xor(position(), k)
                start = pl.multiple_of((h * count + place) * TILE, TILE)
                flat[pl.ds(start, TILE), :] = back_ref[h]
        span = pl.ds(piece * slots // pieces, slots // pieces)
        copies.append(pltpu.make_async_copy(held.at[span], out_hbm.at[span], sems.at[piece]))
        copies[-1].start()
    for copy in copies:
        copy.wait()


def last_kernel(ks, count, highs, gathered_hbm, *rest):
    back_refs, (out_hbm, held, sems) = rest[: len(ks)], rest[len(ks) :]
    _, _, lows, parts, rank = held.shape
    spread = out_hbm.reshape(highs, count * lows, parts, rank)
    flat = held.reshape(len(ks), highs * TILE, rank)
    copies = []
    for at, k in enumerate(ks):
        for h in range(highs):
            flat[at, h * TILE : h * TILE + TILE, :] = back_refs[at][h]
        start = pl.multiple_of(jnp.bitwise_xor(position(), k) * lows, lows)
        place = spread.at[:, pl.ds(start, lows)]
        copies.append(pltpu.make_async_copy(held.at[at], place, sems.at[at]))
        copies[-1].start()
    for copy in copies:
        copy.wait()


def transposed(weights, interp, slowness, box_coord):
    per_dev, parts, rank = weights.shape
    count = lax.axis_size("bx") * lax.axis_size("by")
    half = count // 2
    highs = 1 << LOCAL
    bf16, f32 = jnp.bfloat16, jnp.float32
    vmem = pl.BlockSpec(memory_space=pltpu.VMEM)

    def call(kernel, in_specs, outs, scratch=(), flops=0, moved=0, room=12, place=vmem, alias=None):
        return pl.pallas_call(
            kernel,
            in_specs=in_specs,
            out_specs=[place] * len(outs),
            out_shape=[jax.ShapeDtypeStruct(s, t) for s, t in outs],
            scratch_shapes=list(scratch),
            input_output_aliases=alias or {},
            compiler_params=pltpu.CompilerParams(vmem_limit_bytes=room << 20),
            cost_estimate=pl.CostEstimate(flops=flops, bytes_accessed=moved, transcendentals=0),
        )

    def run(kernel, in_specs, outs, args, **options):
        return call(kernel, in_specs, outs, **options)(*args)

    def swap_with(block, axes, mask):
        size = 1
        for axis in axes:
            size *= lax.axis_size(axis)
        return lax.ppermute(block, axes, [(i, i ^ mask) for i in range(size)])

    other = swap_with(weights, ("bz",), 1)
    (coord,) = run(
        functools.partial(coord_kernel, count, highs),
        [vmem],
        [((count, TILE, rank), bf16)],
        (box_coord,),
        flops=1 << 31,
        moved=1 << 16,
        room=6,
    )
    messages = [None] * count
    raw = run(
        functools.partial(raw_kernel, RAW, count, highs),
        [vmem] * 2,
        [((highs + 1, TILE, rank), bf16)] * len(RAW),
        (weights, coord),
        flops=1 << 24,
        moved=1 << 19,
        room=6,
    )
    others = len(MIXED) - 1
    tile_shape = (highs, TILE, rank)
    own_cos, own_sin, *here = run(
        functools.partial(own_table_kernel, MIXED[1:], highs),
        [vmem] * 2,
        [((others,) + tile_shape, f32)] * 2 + [(tile_shape, f32)] * 4,
        (coord, slowness),
        flops=1 << 31,
        moved=1 << 20,
        room=6,
    )
    mixed = run(
        functools.partial(first_kernel, MIXED, count, highs),
        [vmem] * 8,
        [((highs + 1, TILE, rank), bf16)] * len(MIXED),
        (weights, other, interp, coord, own_cos, own_sin, *here[:2]),
        flops=1 << 27,
        moved=1 << 20,
    )
    for ks, blocks in ((RAW, raw), (MIXED, mixed)):
        for k, block in zip(ks, blocks):
            messages[k] = block
    arrived = [messages[0]] + [swap_with(messages[k], ("bx", "by"), k) for k in range(1, count)]
    tables = [here] + [None] * (count - 1)
    for ks in TABLES:
        outs = run(
            functools.partial(table_kernel, len(ks), highs),
            [vmem] * (len(ks) + 1),
            [(tile_shape, f32)] * (4 * len(ks)),
            (*[arrived[k] for k in ks], slowness),
            flops=1 << 22,
            moved=1 << 19,
            room=6,
        )
        for at, k in enumerate(ks):
            tables[k] = outs[4 * at : 4 * at + 4]
    raised = run(
        functools.partial(raised_kernel, len(RAW), highs),
        [vmem] * (1 + 4 * len(RAW)),
        [(tile_shape, bf16)] * len(RAW),
        (
            interp,
            *[arrived[k] for k in RAW],
            *[swap_with(arrived[k], ("bz",), 1) for k in RAW],
            *[t for k in RAW for t in tables[k][:2]],
        ),
        flops=1 << 27,
        moved=1 << 20,
    )
    for k, block in zip(RAW, raised):
        arrived[k] = block
    halves = []
    for side in range(2):
        ks = range(side * half, side * half + half)
        (done,) = run(
            functools.partial(half_kernel, half, highs),
            [vmem] * (1 + 3 * half),
            [((half,) + tile_shape, f32)],
            (interp, *[arrived[k] for k in ks], *[t for k in ks for t in tables[k][:2]]),
            flops=1 << 29,
            moved=1 << 20,
        )
        halves.append(done)
    results = [None] * count
    for ks in FINALS.values():
        side, size = ks[0] // half, len(ks)
        outs = run(
            functools.partial(
                final_kernel, [k % half for k in ks], highs, count.bit_length() - 2, side
            ),
            [vmem] * (3 + 4 * size),
            [(tile_shape, bf16)] * size,
            (interp, halves[side], halves[1 - side], *[t for k in ks for t in tables[k]]),
            scratch=[pltpu.VMEM((size,) + tile_shape, f32)],
            flops=1 << 29,
            moved=1 << 20,
        )
        for k, out in zip(ks, outs):
            results[k] = out
    back = [results[0]] + [swap_with(results[k], ("bx", "by"), k) for k in range(1, count)]
    early = [k for k in range(count) if k not in LAST]
    whole = ((per_dev, parts, rank), bf16)
    anywhere = pl.BlockSpec(memory_space=pl.ANY)
    (gathered,) = run(
        functools.partial(gather_kernel, early, count, highs),
        [vmem] * len(early),
        [whole],
        [back[k] for k in early],
        scratch=[pltpu.VMEM((per_dev, parts, rank), bf16), pltpu.SemaphoreType.DMA((4,))],
        moved=1 << 20,
        place=anywhere,
    )
    lows = per_dev // highs // count
    (gathered,) = run(
        functools.partial(last_kernel, LAST, count, highs),
        [anywhere] + [vmem] * len(LAST),
        [whole],
        (gathered, *[back[k] for k in LAST]),
        scratch=[
            pltpu.VMEM((len(LAST), highs, lows, parts, rank), bf16),
            pltpu.SemaphoreType.DMA((len(LAST),)),
        ],
        moved=1 << 17,
        place=anywhere,
        alias={0: 0},
    )
    return gathered


def fits(mesh_shape):
    return mesh_shape["bx"] * mesh_shape["by"] == 8 and mesh_shape["bz"] == 2


def local(weights, interp, slowness, box_coord):
    sizes = {axis: lax.axis_size(axis) for axis in ("bx", "by", "bz")}
    if fits(sizes) and weights.shape[0] * weights.shape[1] == (TILE * 8) << LOCAL:
        return transposed(weights, interp, slowness, box_coord)
    return general(weights, interp, slowness, box_coord)


def solution(mesh):
    placed = (P(("shots", "bx", "by", "bz"), None, None), P(), P(), P(None, ("bx", "by", "bz")))
    return jax.shard_map(
        local,
        mesh=mesh,
        in_specs=placed,
        out_specs=P(("shots", "bx", "by", "bz"), None, None),
        check_vma=False,
    )
```

```python
import functools

import jax
import jax.numpy as jnp
from jax import lax
from jax.experimental import pallas as pl
from jax.experimental.pallas import tpu as pltpu
from jax.sharding import PartitionSpec as P


LOCAL = 4
TILE = 8
RAW = (4, 5, 6)
MIXED = (0, 1, 2, 3, 7)
FINALS = {"final_a": (4, 5, 6, 7), "final_c": (1, 2, 3), "final_d": (0,)}
LAST = (4, 3, 2, 1)


def from_partner(block, axis, stride):
    count = lax.axis_size(axis)
    route = []
    for low in range(count):
        high = low | 1 << stride
        if high != low and high < count:
            route += [(low, high), (high, low)]
    return lax.ppermute(block, axis, route)


def apply_matrix(block, matrix):
    block_shape = block.shape
    product = jnp.dot(
        block.reshape(-1, block_shape[-1]), matrix, preferred_element_type=jnp.float32
    )
    return product.reshape(block_shape)


def rotate_phase(summed, cosine, sine):
    real_part = summed[..., 0, :]
    imag_part = summed[..., 1, :]
    return jnp.stack(
        [cosine * real_part - sine * imag_part, sine * real_part + cosine * imag_part], axis=-2
    ).astype(jnp.bfloat16)


def level_step(grouped, interp, cos_group, sin_group):
    first_child = grouped[:, 0]
    second_child = grouped[:, 1]
    results = []
    for target in range(2):
        summed = apply_matrix(first_child, interp[target, 0]) + apply_matrix(
            second_child, interp[target, 1]
        )
        results.append(rotate_phase(summed, cos_group[:, target], sin_group[:, target]))
    return jnp.stack(results, axis=1)


def partner_step(current, partner, upper_bit, interp, cosine, sine):
    mine_part = apply_matrix(current, interp[upper_bit, upper_bit])
    other_part = apply_matrix(partner, interp[upper_bit, 1 - upper_bit])
    return rotate_phase(mine_part + other_part, cosine, sine)


def general(weights, interp, slowness, box_coord):
    per_dev = weights.shape[0]
    rank_size = weights.shape[2]
    coords = box_coord.astype(jnp.float32)
    dist_angle = (
        coords[0][:, None] * slowness[0, 0][None, :] + coords[1][:, None] * slowness[0, 1][None, :]
    )
    local_angle = (
        coords[0][:, None] * slowness[1, 0][None, :] + coords[1][:, None] * slowness[1, 1][None, :]
    )
    dist_cos = jnp.cos(dist_angle)
    dist_sin = jnp.sin(dist_angle)
    local_cos = jnp.cos(local_angle)
    local_sin = jnp.sin(local_angle)
    current = weights
    for axis in ("bz", "by", "bx"):
        for bit_num in range(lax.axis_size(axis).bit_length() - 1):
            partner = from_partner(current, axis, bit_num)
            upper_bit = lax.axis_index(axis) >> bit_num & 1
            current = partner_step(current, partner, upper_bit, interp, dist_cos, dist_sin)
    for local_num in range(LOCAL):
        span_len = per_dev >> local_num + 1
        grouped = current.reshape(-1, 2, span_len, 2, rank_size)
        cos_group = local_cos.reshape(-1, 2, span_len, rank_size)
        sin_group = local_sin.reshape(-1, 2, span_len, rank_size)
        current = level_step(grouped, interp, cos_group, sin_group).reshape(per_dev, 2, rank_size)
    return current


def position():
    return lax.axis_index("bx") * lax.axis_size("by") + lax.axis_index("by")


def rows_of(value):
    return value.reshape(-1, value.shape[-1])


def pick_rows(tiles, rows_from):
    source = rows_from(lax.broadcasted_iota(jnp.int32, tiles.shape[1:], 0))
    return jnp.stack(
        [jnp.take_along_axis(tiles[at], source, axis=0) for at in range(tiles.shape[0])]
    )


def swap_parts(tiles):
    return pick_rows(tiles, lambda row: jnp.bitwise_xor(row, 1))


def rotate_tiles(summed, cosine, sine):
    return cosine * summed + sine * swap_parts(summed)


def even_rows(shape):
    return lax.broadcasted_iota(jnp.int32, shape, len(shape) - 2) % 2 == 0


def sin_cos(angle, flipped):
    quarter = jnp.floor(angle * 0.6366197723675814 + 0.5)
    rest = (angle - quarter * 1.5703125) - quarter * 4.838267948966e-4
    square = rest * rest
    odd_part = (-1.9515295891e-4 * square + 8.3321608736e-3) * square - 1.6666654611e-1
    odd_part = odd_part * (square * rest) + rest
    even_part = (2.443315711809948e-5 * square - 1.388731625493765e-3) * square
    even_part = ((even_part + 4.166664568298827e-2) * square - 0.5) * square + 1.0
    turn = quarter.astype(jnp.int32)
    odd = (turn & 1) != 0
    sine = jnp.where(odd, even_part, odd_part)
    cosine = jnp.where(odd, odd_part, even_part)
    return (
        jnp.where(((turn + flipped) & 2) != 0, -sine, sine),
        jnp.where(((turn + 1) & 2) != 0, -cosine, cosine),
    )


def paired_tables(coords, slow_x, slow_y, count):
    angle = jnp.stack(
        [
            coords[:, h : h + 1] * slow_x + coords[:, count + h : count + h + 1] * slow_y
            for h in range(count)
        ]
    )
    sine, cosine = sin_cos(angle, jnp.where(even_rows(angle.shape), 2, 0))
    sign = jnp.where(even_rows(angle.shape), 1.0, -1.0)

    def even_row(row):
        return row - row % 2

    def odd_row(row):
        return row - row % 2 + 1

    return (
        pick_rows(cosine, even_row),
        pick_rows(sine, even_row) * sign,
        pick_rows(cosine, odd_row),
        pick_rows(sine, odd_row) * -sign,
    )


def coord_kernel(count, highs, box_ref, coord_ref):
    slots = box_ref.shape[1]
    rank = coord_ref.shape[-1]
    wide = 128
    low_count = slots // highs
    rows = count * TILE
    slot = lax.broadcasted_iota(jnp.int32, (rows, slots), 1)
    row = lax.broadcasted_iota(jnp.int32, (rows, slots), 0)
    mine = slot % low_count == row // (rows // low_count)
    high = lax.broadcasted_iota(jnp.int32, (slots, wide), 0) // low_count
    column = lax.broadcasted_iota(jnp.int32, (slots, wide), 1)
    coords = jnp.zeros((rows, wide), jnp.float32)
    for which in range(2):
        picked = jnp.where(mine, box_ref[which : which + 1].astype(jnp.float32), 0.0)
        fold = jnp.where(column == high + which * highs, 1.0, 0.0).astype(jnp.bfloat16)
        coords += jnp.dot(picked.astype(jnp.bfloat16), fold, preferred_element_type=jnp.float32)
    coord_ref[:, :, 0:wide] = coords.reshape(count, TILE, wide).astype(jnp.bfloat16)
    coord_ref[:, :, wide:rank] = jnp.zeros((count, TILE, rank - wide), jnp.bfloat16)


def mixed_slopes(slow_ref):
    even = even_rows((TILE, slow_ref.shape[-1]))
    return [jnp.where(even, slow_ref[0, at : at + 1], slow_ref[1, at : at + 1]) for at in range(2)]


def own_table_kernel(ks, highs, coord_ref, slow_ref, cos_ref, sin_ref, *own_refs):
    rank = coord_ref.shape[-1]
    slow_x = jnp.broadcast_to(slow_ref[0, 0:1], (TILE, rank))
    slow_y = jnp.broadcast_to(slow_ref[0, 1:2], (TILE, rank))

    def coords(k):
        return coord_ref[jnp.bitwise_xor(position(), k)].astype(jnp.float32)

    for out_ref, table in zip(own_refs, paired_tables(coords(0), *mixed_slopes(slow_ref), highs)):
        out_ref[...] = table
    for at in range(0, len(ks), 2):
        two = min(at + 1, len(ks) - 1)
        low, high = coords(ks[at]), coords(ks[two])
        pair = jnp.where(even_rows(low.shape), low, high)
        tables = paired_tables(pair, slow_x, slow_y, highs)
        cos_ref[at], sin_ref[at] = tables[0], tables[1]
        if two != at:
            cos_ref[two], sin_ref[two] = tables[2], tables[3]


def owned(ref, count, highs, k):
    flat = ref.reshape(ref.shape[0] * ref.shape[1], ref.shape[2])
    to = jnp.bitwise_xor(position(), k)
    starts = [pl.multiple_of((h * count + to) * TILE, TILE) for h in range(highs)]
    return [flat[pl.ds(start, TILE), :] for start in starts]


def raw_kernel(ks, count, highs, own_ref, coord_ref, *out_refs):
    for out_ref, k in zip(out_refs, ks):
        for h, tile in enumerate(owned(own_ref, count, highs, k)):
            out_ref[h] = tile
        out_ref[highs] = coord_ref[jnp.bitwise_xor(position(), k)]


def table_kernel(highs, msg_ref, slow_ref, *out_refs):
    coords = msg_ref[highs].astype(jnp.float32)
    for out_ref, table in zip(out_refs, paired_tables(coords, *mixed_slopes(slow_ref), highs)):
        out_ref[...] = table


def mix(near, far, near_matrix, far_matrix):
    return jnp.dot(near, near_matrix, preferred_element_type=jnp.float32) + jnp.dot(
        far, far_matrix, preferred_element_type=jnp.float32
    )


def first_kernel(ks, count, highs, own_ref, other_ref, interp_ref, coord_ref, *rest):
    cos_ref, sin_ref, here_cos_ref, here_sin_ref = rest[:4]
    out_refs = rest[4:]
    upper = lax.axis_index("bz")
    rank = own_ref.shape[-1]
    blocks = [
        jnp.concatenate([tile for k in ks for tile in owned(ref, count, highs, k)])
        for ref in (own_ref, other_ref)
    ]
    summed = mix(*blocks, interp_ref[upper, upper], interp_ref[upper, 1 - upper])
    summed = summed.reshape(len(ks), highs, TILE, rank)
    for at, k in enumerate(ks):
        tables = (here_cos_ref[...], here_sin_ref[...]) if k == 0 else (cos_ref[at - 1], sin_ref[at - 1])
        turned = rotate_tiles(summed[at], *tables)
        out_refs[at][0:highs] = turned.astype(jnp.bfloat16)
        out_refs[at][highs] = coord_ref[jnp.bitwise_xor(position(), k)]


def raised_kernel(size, highs, interp_ref, *rest):
    own_refs, other_refs, rest = rest[:size], rest[size : 2 * size], rest[2 * size :]
    table_refs, out_refs = rest[: 2 * size], rest[2 * size :]
    upper = lax.axis_index("bz")
    rank = interp_ref.shape[-1]
    own, other = [
        jnp.concatenate([rows_of(ref[0:highs].astype(jnp.float32)) for ref in refs])
        for refs in (own_refs, other_refs)
    ]
    summed = mix(
        own.astype(jnp.bfloat16),
        other.astype(jnp.bfloat16),
        interp_ref[upper, upper],
        interp_ref[upper, 1 - upper],
    ).reshape(size, highs, TILE, rank)
    for k in range(size):
        turned = rotate_tiles(summed[k], table_refs[2 * k][...], table_refs[2 * k + 1][...])
        out_refs[k][...] = turned.astype(jnp.bfloat16)


def device_level(children, upper, interp_ref):
    return [
        mix(children[t], children[1 - t], interp_ref[u, u], interp_ref[u, 1 - u])
        for t, u in ((0, upper), (1, 1 - upper))
    ]


def half_kernel(size, highs, interp_ref, *rest):
    msg_refs, table_refs, out_ref = rest[:size], rest[size : 3 * size], rest[3 * size]
    rank = interp_ref.shape[-1]
    bits = size.bit_length() - 1
    held = [rows_of(msg_refs[k][0:highs].astype(jnp.float32)).astype(jnp.bfloat16) for k in range(size)]
    for bit in range(bits):
        mine = jnp.right_shift(position(), bit) & 1
        groups = [[k for k in range(size) if k >> bit & 1 == t] for t in range(2)]
        children = [jnp.concatenate([held[k] for k in ks]) for ks in groups]
        for ks, summed in zip(groups, device_level(children, mine, interp_ref)):
            summed = summed.reshape(len(ks), highs, TILE, rank)
            for at, k in enumerate(ks):
                turned = rotate_tiles(summed[at], table_refs[2 * k][...], table_refs[2 * k + 1][...])
                if bit == bits - 1:
                    out_ref[k] = turned
                else:
                    held[k] = rows_of(turned).astype(jnp.bfloat16)


def final_kernel(places, highs, last_bit, flip, interp_ref, near_ref, other_ref, *rest):
    size = len(places)
    table_refs, out_refs, held = rest[: 4 * size], rest[4 * size : 5 * size], rest[5 * size]
    rank = interp_ref.shape[-1]
    upper = jnp.bitwise_xor(jnp.right_shift(position(), last_bit) & 1, flip)
    near, other = [
        jnp.concatenate([rows_of(ref[at]) for at in places]).astype(jnp.bfloat16)
        for ref in (near_ref, other_ref)
    ]
    summed = mix(near, other, interp_ref[upper, upper], interp_ref[upper, 1 - upper])
    summed = summed.reshape(size, highs, TILE, rank)
    for at in range(size):
        cos_ref, sin_ref = table_refs[4 * at : 4 * at + 2]
        held[at] = rotate_tiles(summed[at], cos_ref[...], sin_ref[...])
    for level in range(LOCAL):
        span = highs >> level + 1
        groups = [[h for h in range(highs) if (h // span) % 2 == t] for t in range(2)]
        children = []
        for t in range(2):
            tiles = [held[at, h] for at in range(size) for h in groups[t]]
            children.append(jnp.concatenate(tiles).astype(jnp.bfloat16))
        for t in range(2):
            summed = mix(children[0], children[1], interp_ref[t, 0], interp_ref[t, 1])
            summed = summed.reshape(size, highs // 2, TILE, rank)
            for at in range(size):
                cos_ref, sin_ref = table_refs[4 * at + 2 : 4 * at + 4]
                cosine = jnp.stack([cos_ref[h] for h in groups[t]])
                sine = jnp.stack([sin_ref[h] for h in groups[t]])
                turned = rotate_tiles(summed[at], cosine, sine)
                for place, h in enumerate(groups[t]):
                    if level == LOCAL - 1:
                        out_refs[at][h] = turned[place].astype(jnp.bfloat16)
                    else:
                        held[at, h] = turned[place]


def gather_kernel(ks, count, highs, *rest):
    back_refs, (out_hbm, held, sems) = rest[: len(ks)], rest[len(ks) :]
    slots, parts, rank = held.shape
    flat = held.reshape(slots * parts, rank)
    pieces = sems.shape[0]
    copies = []
    for piece in range(pieces):
        for h in range(piece * highs // pieces, (piece + 1) * highs // pieces):
            for back_ref, k in zip(back_refs, ks):
                place = jnp.bitwise_xor(position(), k)
                start = pl.multiple_of((h * count + place) * TILE, TILE)
                flat[pl.ds(start, TILE), :] = back_ref[h]
        span = pl.ds(piece * slots // pieces, slots // pieces)
        copies.append(pltpu.make_async_copy(held.at[span], out_hbm.at[span], sems.at[piece]))
        copies[-1].start()
    for copy in copies:
        copy.wait()


def last_kernel(ks, count, highs, gathered_hbm, *rest):
    back_refs, (out_hbm, held, sems) = rest[: len(ks)], rest[len(ks) :]
    _, _, lows, parts, rank = held.shape
    spread = out_hbm.reshape(highs, count * lows, parts, rank)
    flat = held.reshape(len(ks), highs * TILE, rank)
    copies = []
    for at, k in enumerate(ks):
        for h in range(highs):
            flat[at, h * TILE : h * TILE + TILE, :] = back_refs[at][h]
        start = pl.multiple_of(jnp.bitwise_xor(position(), k) * lows, lows)
        place = spread.at[:, pl.ds(start, lows)]
        copies.append(pltpu.make_async_copy(held.at[at], place, sems.at[at]))
        copies[-1].start()
    for copy in copies:
        copy.wait()


def transposed(weights, interp, slowness, box_coord):
    per_dev, parts, rank = weights.shape
    count = lax.axis_size("bx") * lax.axis_size("by")
    half = count // 2
    highs = 1 << LOCAL
    bf16, f32 = jnp.bfloat16, jnp.float32
    vmem = pl.BlockSpec(memory_space=pltpu.VMEM)

    def call(kernel, in_specs, outs, scratch=(), flops=0, moved=0, room=12, place=vmem, alias=None):
        return pl.pallas_call(
            kernel,
            in_specs=in_specs,
            out_specs=[place] * len(outs),
            out_shape=[jax.ShapeDtypeStruct(s, t) for s, t in outs],
            scratch_shapes=list(scratch),
            input_output_aliases=alias or {},
            compiler_params=pltpu.CompilerParams(vmem_limit_bytes=room << 20),
            cost_estimate=pl.CostEstimate(flops=flops, bytes_accessed=moved, transcendentals=0),
        )

    def run(kernel, in_specs, outs, args, **options):
        return call(kernel, in_specs, outs, **options)(*args)

    def swap_with(block, axes, mask):
        size = 1
        for axis in axes:
            size *= lax.axis_size(axis)
        return lax.ppermute(block, axes, [(i, i ^ mask) for i in range(size)])

    other = swap_with(weights, ("bz",), 1)
    (coord,) = run(
        functools.partial(coord_kernel, count, highs),
        [vmem],
        [((count, TILE, rank), bf16)],
        (box_coord,),
        flops=1 << 31,
        moved=1 << 16,
        room=6,
    )
    messages = [None] * count
    raw = run(
        functools.partial(raw_kernel, RAW, count, highs),
        [vmem] * 2,
        [((highs + 1, TILE, rank), bf16)] * len(RAW),
        (weights, coord),
        flops=1 << 24,
        moved=1 << 19,
        room=6,
    )
    others = len(MIXED) - 1
    tile_shape = (highs, TILE, rank)
    own_cos, own_sin, *here = run(
        functools.partial(own_table_kernel, MIXED[1:], highs),
        [vmem] * 2,
        [((others,) + tile_shape, f32)] * 2 + [(tile_shape, f32)] * 4,
        (coord, slowness),
        flops=1 << 31,
        moved=1 << 20,
        room=6,
    )
    mixed = run(
        functools.partial(first_kernel, MIXED, count, highs),
        [vmem] * 8,
        [((highs + 1, TILE, rank), bf16)] * len(MIXED),
        (weights, other, interp, coord, own_cos, own_sin, *here[:2]),
        flops=1 << 27,
        moved=1 << 20,
    )
    for ks, blocks in ((RAW, raw), (MIXED, mixed)):
        for k, block in zip(ks, blocks):
            messages[k] = block
    arrived = [messages[0]] + [swap_with(messages[k], ("bx", "by"), k) for k in range(1, count)]
    tables = [here] + [None] * (count - 1)
    for k in range(1, count):
        tables[k] = run(
            functools.partial(table_kernel, highs),
            [vmem, vmem],
            [((highs, TILE, rank), f32)] * 4,
            (arrived[k], slowness),
            flops=1 << 22,
            moved=1 << 19,
            room=6,
        )
    raised = run(
        functools.partial(raised_kernel, len(RAW), highs),
        [vmem] * (1 + 4 * len(RAW)),
        [(tile_shape, bf16)] * len(RAW),
        (
            interp,
            *[arrived[k] for k in RAW],
            *[swap_with(arrived[k], ("bz",), 1) for k in RAW],
            *[t for k in RAW for t in tables[k][:2]],
        ),
        flops=1 << 27,
        moved=1 << 20,
    )
    for k, block in zip(RAW, raised):
        arrived[k] = block
    halves = []
    for side in range(2):
        ks = range(side * half, side * half + half)
        (done,) = run(
            functools.partial(half_kernel, half, highs),
            [vmem] * (1 + 3 * half),
            [((half,) + tile_shape, f32)],
            (interp, *[arrived[k] for k in ks], *[t for k in ks for t in tables[k][:2]]),
            flops=1 << 29,
            moved=1 << 20,
        )
        halves.append(done)
    results = [None] * count
    for ks in FINALS.values():
        side, size = ks[0] // half, len(ks)
        outs = run(
            functools.partial(
                final_kernel, [k % half for k in ks], highs, count.bit_length() - 2, side
            ),
            [vmem] * (3 + 4 * size),
            [(tile_shape, bf16)] * size,
            (interp, halves[side], halves[1 - side], *[t for k in ks for t in tables[k]]),
            scratch=[pltpu.VMEM((size,) + tile_shape, f32)],
            flops=1 << 29,
            moved=1 << 20,
        )
        for k, out in zip(ks, outs):
            results[k] = out
    back = [results[0]] + [swap_with(results[k], ("bx", "by"), k) for k in range(1, count)]
    early = [k for k in range(count) if k not in LAST]
    whole = ((per_dev, parts, rank), bf16)
    anywhere = pl.BlockSpec(memory_space=pl.ANY)
    (gathered,) = run(
        functools.partial(gather_kernel, early, count, highs),
        [vmem] * len(early),
        [whole],
        [back[k] for k in early],
        scratch=[pltpu.VMEM((per_dev, parts, rank), bf16), pltpu.SemaphoreType.DMA((4,))],
        moved=1 << 20,
        place=anywhere,
    )
    lows = per_dev // highs // count
    (gathered,) = run(
        functools.partial(last_kernel, LAST, count, highs),
        [anywhere] + [vmem] * len(LAST),
        [whole],
        (gathered, *[back[k] for k in LAST]),
        scratch=[
            pltpu.VMEM((len(LAST), highs, lows, parts, rank), bf16),
            pltpu.SemaphoreType.DMA((len(LAST),)),
        ],
        moved=1 << 17,
        place=anywhere,
        alias={0: 0},
    )
    return gathered


def fits(mesh_shape):
    return mesh_shape["bx"] * mesh_shape["by"] == 8 and mesh_shape["bz"] == 2


def local(weights, interp, slowness, box_coord):
    sizes = {axis: lax.axis_size(axis) for axis in ("bx", "by", "bz")}
    if fits(sizes) and weights.shape[0] * weights.shape[1] == (TILE * 8) << LOCAL:
        return transposed(weights, interp, slowness, box_coord)
    return general(weights, interp, slowness, box_coord)


def solution(mesh):
    placed = (P(("shots", "bx", "by", "bz"), None, None), P(), P(), P(None, ("bx", "by", "bz")))
    return jax.shard_map(
        local,
        mesh=mesh,
        in_specs=placed,
        out_specs=P(("shots", "bx", "by", "bz"), None, None),
        check_vma=False,
    )
```
